512 devices in a mesh: dp: 8 (over y), seq: 64 (over z, x, core).
Axes of the slice: x: 4, y: 8, z: 8, core: 2. Of those that a mesh axis runs over, the one named last changes fastest.
Arguments:
- mel_frames: bfloat16 [8, 16384, 128], P('dp', 'seq'), may hold values from -16 to 16
- positions: int32 [8, 8192], P('dp', 'seq'), may hold values from 0 to 16383, as said below
- conv_weight: bfloat16 [128, 3, 1280], replicated, may hold values from -0.3125 to 0.3125
- conv_bias: float32 [1280], replicated, may hold values from -3 to 3
- proj_weight: bfloat16 [1280, 2048], P('dp'), may hold values from -0.15625 to 0.15625
- proj_bias: float32 [2048], replicated, may hold values from -3 to 3
- cotangent: bfloat16 [8, 16384, 2048], P('dp', 'seq'), may hold values from -0.032958984 to 0.032958984
Outputs:
- merged: bfloat16 [8, 16384, 2048], P('dp', 'seq')
- grad_weight: float32 [128, 3, 1280], P('seq', None, 'dp')
The draws below stay inside these ranges and needn't reach their ends.
Inputs may be any that keep to these rules, and one draw needn't show every extreme that they name: Within a recording the 8192 entries are distinct. Block b of the sequence is positions b * 256 to b * 256 + 255; the 128 tokens of one window put at most 4 entries into any one block, and in each recording one block receives exactly 4 from every window.
All inputs are finite; a program needn't handle non-finite values.
Results may differ from the reference program's by a relative error of at most 0.012.
Values may be sent and summed in bfloat16 or wider, within the bound.
A program may use at most 64 MiB of HBM per device.

```python
import jax
import jax.numpy as jnp
from jax import lax

NMEL = 128
KW = 3
CH = 1280
D = 2048
FRAMES = 256
TOK = 128
CAP = 4
ROWS_OWN = 256
RECS = 8
SEQ_FRAMES = 16384
TOKENS = 8192
SEQ_LEN = 16384
ALL_FRAMES = 131072
N_DP = 8
N_SEQ = 64


def owner_permutation(row_key):
    return jax.random.permutation(row_key, ROWS_OWN).astype(jnp.int32)


def record_positions(record_key):
    key_full, key_rows, key_sources = jax.random.split(record_key, 3)
    full_owner = jax.random.randint(key_full, (), 0, N_SEQ).astype(jnp.int32)
    slot_total = N_SEQ * CAP
    slot_ids = jnp.arange(slot_total, dtype=jnp.int32)
    slot_owner = slot_ids // CAP
    row_tables = jax.vmap(owner_permutation)(jax.random.split(key_rows, N_SEQ))
    source_keys = jax.random.split(key_sources, N_SEQ)

    def one_source(source_index, source_key):
        key_scores, key_order = jax.random.split(source_key)
        scores = jax.random.permutation(key_scores, slot_total).astype(jnp.int32)
        scores = jnp.where(slot_owner == full_owner, slot_ids - slot_total, scores)
        sorted_slots = jnp.argsort(scores).astype(jnp.int32)
        kept_slots = sorted_slots[:TOK]
        kept_slots = kept_slots[jax.random.permutation(key_order, TOK)]
        owners = kept_slots // CAP
        local_slot = source_index * CAP + kept_slots % CAP
        owner_rows = row_tables[owners, local_slot]
        return owners * ROWS_OWN + owner_rows
    result = jax.vmap(one_source)(jnp.arange(N_SEQ, dtype=jnp.int32), source_keys)
    return result.reshape(-1)


def draw_positions(key, part):
    record_keys = jax.random.split(key, N_DP)
    return jax.vmap(record_positions)(record_keys).astype(jnp.int32)


def with_spikes(drawn, rng, source, target, parts, factor):
    owner, partner = [(jnp.arange(drawn.shape[axis_at]) // (drawn.shape[axis_at] // parts)).reshape([-1 if axis == axis_at else 1 for axis in range(drawn.ndim)]) for axis_at in (source, target)]
    chosen = jax.random.permutation(rng, parts)[partner]
    strong = (owner == chosen) | (owner == (partner + parts // 2) % parts)
    return jnp.where(strong, factor * drawn, drawn)


def level_of(key, shape, cuts, low, high):
    def one(position, shards_of):
        heights = jax.random.uniform(jax.random.fold_in(jax.random.fold_in(key, 6), position), (shards_of,), jnp.float32, low / len(cuts), high / len(cuts))
        return jnp.repeat(jnp.exp(heights), shape[position] // shards_of).reshape((-1,) + (1,) * (len(shape) - position - 1))

    gain = one(*cuts[0])
    for cut in cuts[1:]:
        gain = gain * one(*cut)
    return gain


def scatter_about(own_key, extent, spread, reach, pieces=(), held_as=jnp.bfloat16):
    values = spread * jax.random.normal(own_key, extent, jnp.float32)
    if pieces:
        values = values * level_of(own_key, extent, pieces, -0.22, 0.18)
    return jnp.clip(values, -reach, reach).astype(held_as)


def noise_with(rng, extent, deviation, most, cuts, heavy, kind=jnp.bfloat16):
    drawn = deviation * jax.random.normal(rng, extent, jnp.float32)
    if cuts:
        drawn = drawn * level_of(rng, extent, cuts, -0.22, 0.18)
    return jnp.clip(with_spikes(drawn, jax.random.fold_in(rng, 3), *heavy), -most, most).astype(kind)


def setup_inputs(seed: int = 0) -> dict:
    keys = jax.random.split(jax.random.key(seed), 8)
    mel_frames = noise_with(keys[0], (RECS, SEQ_FRAMES, NMEL), 1.0, 16.0, ((0, 8), (1, 64)), (1, 2, 64, 4.0))
    positions = draw_positions(jax.random.fold_in(keys[7], 71), 0)
    conv_weight = scatter_about(keys[2], (NMEL, KW, CH), (NMEL * KW) ** -0.5, 0.3125)
    conv_bias = scatter_about(keys[3], (CH,), 0.5, 3.0, (), jnp.float32)
    proj_weight = scatter_about(keys[4], (CH, D), CH ** -0.5, 0.15625, ((0, 8),))
    proj_bias = scatter_about(keys[5], (D,), 0.5, 3.0, (), jnp.float32)
    cotangent = scatter_about(keys[6], (RECS, SEQ_LEN, D), (2.0 / ALL_FRAMES ** 0.5), 0.032958984, ((0, 8), (1, 64)))
    return {"mel_frames": mel_frames, "positions": positions, "conv_weight": conv_weight, "conv_bias": conv_bias, "proj_weight": proj_weight, "proj_bias": proj_bias, "cotangent": cotangent}


SQRT_HALF = 0.7071067811865476
INV_SQRT_TWO_PI = 0.3989422804014327


def gelu_value(x):
    return x * 0.5 * (1.0 + lax.erf(x * SQRT_HALF))


def gelu_slope(x):
    return 0.5 * (1.0 + lax.erf(x * SQRT_HALF)) + x * INV_SQRT_TWO_PI * jnp.exp(-0.5 * x * x)


def reference(mel_frames, positions, conv_weight, conv_bias, proj_weight, proj_bias, cotangent):
    kernel = jnp.transpose(conv_weight, (1, 0, 2)).reshape(KW * NMEL, CH)

    def one_record(record_args):
        frames, token_spots, grads_in = record_args
        windows = frames.reshape(N_SEQ, FRAMES, NMEL)
        padded = jnp.pad(windows, ((0, 0), (1, 1), (0, 0)))
        stacked = jnp.concatenate([padded[:, k:k + FRAMES, :] for k in range(KW)], axis=2)
        stacked = stacked.reshape(N_SEQ * FRAMES, KW * NMEL)
        pre_act = jnp.dot(stacked, kernel, preferred_element_type=jnp.float32) + conv_bias
        act_pairs = gelu_value(pre_act).reshape(TOKENS, 2, CH)
        pooled = (0.5 * (act_pairs[:, 0, :] + act_pairs[:, 1, :])).astype(jnp.bfloat16)
        projected = (jnp.dot(pooled, proj_weight, preferred_element_type=jnp.float32) + proj_bias).astype(jnp.bfloat16)
        merged = jnp.zeros((SEQ_LEN, D), jnp.bfloat16).at[token_spots].set(projected)
        grad_tokens = jnp.take(grads_in, token_spots, axis=0)
        grad_pooled = jnp.dot(grad_tokens, proj_weight.T, preferred_element_type=jnp.float32).astype(jnp.bfloat16)
        slopes = gelu_slope(pre_act).reshape(TOKENS, 2, CH)
        grad_pre = (0.5 * grad_pooled.astype(jnp.float32)[:, None, :] * slopes).astype(jnp.bfloat16)
        grad_pre = grad_pre.reshape(N_SEQ * FRAMES, CH)
        tap_terms = []
        for k in range(KW):
            shifted = padded[:, k:k + FRAMES, :].reshape(N_SEQ * FRAMES, NMEL)
            tap_terms.append(jnp.dot(shifted.T, grad_pre, preferred_element_type=jnp.float32))
        return merged, jnp.stack(tap_terms, axis=1)

    merged, record_terms = lax.map(one_record, (mel_frames, positions, cotangent))
    return merged, jnp.sum(record_terms, axis=0)
```

```python
import jax
import jax.numpy as jnp
from jax import lax
from jax.sharding import PartitionSpec as P

SQRT_HALF = 0.7071067811865476
INV_SQRT_TWO_PI = 0.3989422804014327


def body(mel_frames, positions, conv_weight, conv_bias, proj_weight, proj_bias, cotangent):
    frames = mel_frames[0]
    spots = positions[0]
    grads_in = cotangent[0]
    n_own = lax.axis_size("seq")
    n_dp = lax.axis_size("dp")
    frame_count, mels = frames.shape
    tok = frame_count // 2
    rows_own, feats = grads_in.shape
    cap = rows_own // n_own
    taps = conv_weight.shape[1]
    ch = conv_weight.shape[2]
    f32, bf16 = jnp.float32, jnp.bfloat16

    full_weight = lax.all_gather(proj_weight, "dp", axis=0, tiled=True)
    padded = jnp.pad(frames, ((1, 1), (0, 0)))
    pairs = padded.reshape(tok + 1, 2 * mels)
    windows = jnp.concatenate([pairs[:-1], pairs[1:]], axis=1)
    owner = spots // rows_own
    row = (spots % rows_own).astype(bf16)
    extra = jnp.concatenate([row[:, None] + 1, jnp.zeros((tok, mels - 1), bf16)], axis=1)
    payload = jnp.concatenate([windows, extra], axis=1)
    earlier = jnp.arange(tok)[None, :] < jnp.arange(tok)[:, None]
    rank = jnp.sum((owner[:, None] == owner[None, :]) & earlier, axis=1)
    slot = owner * cap + rank
    place = (jnp.arange(n_own * cap)[:, None] == slot[None, :]).astype(bf16)
    outgoing = jnp.dot(place, payload, preferred_element_type=f32).astype(bf16)
    arrived = lax.all_to_all(
        outgoing.reshape(n_own, cap, -1), "seq", split_axis=0, concat_axis=0, tiled=True
    ).reshape(n_own * cap, -1)
    arrived_row = arrived[:, 4 * mels].astype(jnp.int32) - 1
    pick = jnp.arange(rows_own)[:, None] == arrived_row[None, :]
    used = jnp.any(pick, axis=1)
    x = jnp.dot(pick.astype(bf16), arrived[:, : 4 * mels], preferred_element_type=f32).astype(bf16)
    kernel = jnp.transpose(conv_weight, (1, 0, 2)).reshape(taps * mels, ch)
    x0, x1 = x[:, : taps * mels], x[:, mels:]
    pre0 = jnp.dot(x0, kernel, preferred_element_type=f32) + conv_bias
    pre1 = jnp.dot(x1, kernel, preferred_element_type=f32) + conv_bias
    phi0 = 0.5 * (1.0 + lax.erf(pre0 * SQRT_HALF))
    phi1 = 0.5 * (1.0 + lax.erf(pre1 * SQRT_HALF))
    pooled = (0.5 * (pre0 * phi0 + pre1 * phi1)).astype(bf16)
    slope0 = phi0 + pre0 * INV_SQRT_TWO_PI * jnp.exp(-0.5 * pre0 * pre0)
    slope1 = phi1 + pre1 * INV_SQRT_TWO_PI * jnp.exp(-0.5 * pre1 * pre1)
    contract_last = (((1,), (1,)), ((), ()))
    grad_pooled = (
        lax.dot_general(grads_in, full_weight, contract_last, preferred_element_type=f32)
        .astype(bf16)
        .astype(f32)
    )
    g0 = (0.5 * grad_pooled * slope0).astype(bf16)
    g1 = (0.5 * grad_pooled * slope1).astype(bf16)
    contract_first = (((0,), (0,)), ((), ()))
    part = lax.dot_general(x0, g0, contract_first, preferred_element_type=f32) + lax.dot_general(
        x1, g1, contract_first, preferred_element_type=f32
    )
    part = part.astype(bf16).reshape(taps, n_own, mels // n_own, ch)
    part = jnp.transpose(part, (1, 2, 0, 3)).reshape(n_own, -1, ch)
    part = lax.all_to_all(part, "seq", split_axis=0, concat_axis=0, tiled=True)
    part = jnp.sum(part.astype(f32), axis=0).astype(bf16)
    part = jnp.transpose(part.reshape(-1, n_dp, ch // n_dp), (1, 0, 2))
    part = lax.all_to_all(part, "dp", split_axis=0, concat_axis=0, tiled=True)
    grad_weight = jnp.sum(part.astype(f32), axis=0).reshape(mels // n_own, taps, ch // n_dp)
    projected = jnp.dot(pooled, full_weight, preferred_element_type=f32) + proj_bias
    merged = jnp.where(used[:, None], projected, 0.0).astype(bf16)
    return (merged[None], grad_weight)


def solution(mesh):
    in_specs = (
        P("dp", "seq", None),
        P("dp", "seq"),
        P(),
        P(),
        P("dp", None),
        P(),
        P("dp", "seq", None),
    )
    out_specs = (P("dp", "seq", None), P("seq", None, "dp"))
    return jax.shard_map(body, mesh=mesh, in_specs=in_specs, out_specs=out_specs, check_vma=False)
```

```python
import functools

import jax
import jax.numpy as jnp
from jax import lax
from jax.experimental import pallas as pl
from jax.experimental.pallas import tpu as pltpu
from jax.sharding import PartitionSpec as P

SQRT_HALF = 0.7071067811865476
INV_SQRT_TWO_PI = 0.3989422804014327
F32, BF16, I32 = jnp.float32, jnp.bfloat16, jnp.int32
MESH = pl.DeviceIdType.MESH
NT = (((1,), (1,)), ((), ()))
NX, NC = 4, 2


def mo(value, k):
    return pl.multiple_of(value, k)


def kernel(
    ny,
    ns,
    nx,
    mel_ref,
    pos_ref,
    kt_ref,
    bias_ref,
    w_ref,
    pbias_ref,
    cot_ref,
    merged_ref,
    gw_ref,
    wf,
    cot2,
    kt,
    biast,
    msgs,
    arr,
    posv,
    fr,
    xt,
    pt,
    pts,
    ptr,
    slope,
    gt,
    zsend,
    zrecv,
    ysend,
    yrecv,
    xsend,
    xrecv,
    mscr,
    ring_send,
    ring_recv,
    sib_send,
    sib_recv,
    pos_sem,
    msg_sem,
    cot_sem,
    fr_sem,
    pt_sem,
    z_sem,
    y_sem,
    x_sem,
    loc_sem,
):
    nq = nx * NC
    nz = ns // nq
    frames, mels = mel_ref.shape
    tok = frames // 2
    rows = cot_ref.shape[0]
    feats = wf.shape[1]
    ch = wf.shape[0]
    shard = ch // ny
    half = shard // NC
    lp = gt.shape[0] // 2
    cap = rows // ns
    mr = 4 * cap
    km = kt.shape[1]
    taps = km // mels
    mz = mels // nz
    zr = km // nz
    mper = mels // ns

    y = lax.axis_index("dp")
    s = lax.axis_index("seq")
    c = lax.rem(s, NC)
    q = lax.rem(s, nq)
    z = s // nq
    sib = s + 1 - 2 * c
    up, down = lax.rem(y + 1, ny), lax.rem(y + ny - 1, ny)

    def remote(src, dst, ssem, rsem, dev):
        return pltpu.make_async_remote_copy(
            src_ref=src, dst_ref=dst, send_sem=ssem, recv_sem=rsem, device_id=dev, device_id_type=MESH
        )

    def drain(ref, sem):
        pltpu.make_async_copy(ref, ref, sem).wait()

    barrier = pltpu.get_barrier_semaphore()

    def hail_seq(i, carry):
        pl.semaphore_signal(barrier, inc=1, device_id=(y, lax.rem(s + i, ns)), device_id_type=MESH)
        return carry

    def hail_dp(i, carry):
        pl.semaphore_signal(barrier, inc=1, device_id=(lax.rem(y + i, ny), s), device_id_type=MESH)
        return carry

    lax.fori_loop(1, ny, hail_dp, 0)
    lax.fori_loop(1, ns, hail_seq, 0)

    own_w = pltpu.make_async_copy(w_ref, wf.at[pl.ds(mo(y * shard, 16), shard)], loc_sem.at[0])
    own_w.start()
    own_cot = pltpu.make_async_copy(cot_ref, cot2.at[pl.ds(0, rows)], loc_sem.at[1])
    own_cot.start()
    own_kt = pltpu.make_async_copy(kt_ref, kt, loc_sem.at[2])
    own_kt.start()

    before = (
        lax.broadcasted_iota(I32, (tok, tok), 0) < lax.broadcasted_iota(I32, (tok, tok), 1)
    ).astype(BF16)
    total = ns * mr

    def spread(hit, value):
        hit_b = hit.astype(F32).astype(BF16)
        rank = jnp.dot(hit_b, before, preferred_element_type=F32)
        lane = lax.broadcasted_iota(I32, (ns, 128), 1)
        table = jnp.zeros((ns, 128), F32)
        for k in range(cap):
            entry = jnp.sum(jnp.where(hit & (rank == k), value + 1.0, 0.0), axis=1, keepdims=True)
            table = table + jnp.where(lane == k, entry, 0.0)
        group = lax.broadcasted_iota(I32, (total, ns), 0) // mr
        expand = (group == lax.broadcasted_iota(I32, (total, ns), 1)).astype(F32).astype(BF16)
        wide = jnp.dot(expand, table.astype(BF16), preferred_element_type=F32)
        n = lax.broadcasted_iota(I32, (total, 128), 0)
        chosen = lax.broadcasted_iota(I32, (total, 128), 1) == lax.rem(n // 4, cap)
        return jnp.sum(jnp.where(chosen, wide, 0.0), axis=1, keepdims=True)

    pos_row = jnp.broadcast_to(pos_ref[...], (ns, tok))
    to_dest = (pos_row // rows) == lax.broadcasted_iota(I32, (ns, tok), 0)
    token = spread(to_dest, lax.broadcasted_iota(I32, (ns, tok), 1).astype(F32))
    n_col = lax.broadcasted_iota(I32, (total, 1), 0)
    f_col = lax.rem(n_col, 4).astype(F32)
    frame = jnp.where(token > 0.0, 2.0 * (token - 1.0) - 1.0 + f_col, -100.0)
    pick = (lax.broadcasted_iota(I32, (total, frames), 1).astype(F32) == frame).astype(F32)
    msgs[...] = jnp.dot(pick.astype(BF16), mel_ref[...], preferred_element_type=F32).astype(BF16)
    own_slot = pl.ds(mo(s * mr, 16), mr)
    arr[own_slot, :] = msgs[own_slot, :]
    posv[s] = pos_ref[...]

    for i in range(ch // 128):
        block = jnp.broadcast_to(bias_ref[:, 128 * i : 128 * (i + 1)], (128, 128))
        biast[128 * i : 128 * (i + 1), :] = jnp.transpose(block)
    gt[...] = jnp.zeros_like(gt)

    pl.semaphore_wait(barrier, ny + ns - 2)

    far = ny // 2
    cut = -(-(half // 2) // 16) * 16

    def wrows(owner, lo, size):
        return wf.at[pl.ds(mo(owner * shard + c * half + lo, 16), size)]

    def ring(step, way):
        owner = lax.rem(y + ny + 1 - step if way == 0 else y + step - 1, ny)
        if step < far:
            lo, size = 0, half
        else:
            lo, size = (0, cut) if way == 0 else (cut, half - cut)
        if step == 1:
            src = w_ref.at[pl.ds(mo(c * half + lo, 16), size)]
        else:
            src = wrows(owner, lo, size)
        target = (up, s) if way == 0 else (down, s)
        i = way * far + step - 1
        return remote(src, wrows(owner, lo, size), ring_send.at[i], ring_recv.at[i], target)

    def came(step, way):
        owner = lax.rem(y + ny - step if way == 0 else y + step, ny)
        if step < far:
            lo, size = 0, half
        else:
            lo, size = (0, cut) if way == 0 else (cut, half - cut)
        return wrows(owner, lo, size)

    def to_sibling(step, way):
        part = came(step, way)
        return remote(part, part, sib_send, sib_recv, (y, sib))

    def serve(step):
        for way in (0, 1):
            part = came(step, way)
            pltpu.make_async_copy(part, part, ring_recv.at[way * far + step - 1]).wait()
            if step < far:
                ring(step + 1, way).start()
            to_sibling(step, way).start()

    ring(1, 0).start()
    ring(1, 1).start()

    def post(i, carry):
        to = lax.rem(s + i, ns)
        remote(posv.at[s], posv.at[s], pos_sem.at[0], pos_sem.at[1], (y, to)).start()
        remote(
            msgs.at[pl.ds(mo(to * mr, 16), mr)],
            arr.at[pl.ds(mo(s * mr, 16), mr)],
            msg_sem.at[0],
            msg_sem.at[1],
            (y, to),
        ).start()
        return carry

    lax.fori_loop(1, ns, post, 0)
    send_cot = remote(
        cot_ref, cot2.at[pl.ds(rows, rows)], cot_sem.at[0], cot_sem.at[1], (y, sib)
    )
    send_cot.start()

    drain(posv.at[pl.ds(0, ns - 1)], pos_sem.at[1])
    all_pos = jnp.reshape(posv[...], (ns, tok))
    mine = (all_pos // rows) == s
    slot_row = spread(mine, lax.rem(all_pos, rows).astype(F32)) - 1.0
    row_lane = lax.broadcasted_iota(I32, (total, rows), 1).astype(F32)
    at_row = row_lane == slot_row
    n_f = lax.rem(lax.broadcasted_iota(I32, (total, rows), 0), 4)
    places = [(at_row & (n_f == f)).astype(F32).astype(BF16) for f in range(4)]
    used = lax.dot_general(
        places[0], jnp.ones((total, 128), BF16), (((0,), (0,)), ((), ())), preferred_element_type=F32
    )
    drain(arr.at[pl.ds(0, (ns - 1) * mr)], msg_sem.at[1])
    arr_t = jnp.transpose(arr[...])
    for f in range(4):
        fr[f, :, 0:rows] = jnp.dot(arr_t, places[f], preferred_element_type=F32).astype(BF16)
    send_fr = remote(
        fr.at[:, :, pl.ds(0, rows)], fr.at[:, :, pl.ds(rows, rows)], fr_sem.at[0], fr_sem.at[1], (y, sib)
    )
    send_fr.start()
    if far > 1:
        serve(1)
    own_kt.wait()
    send_fr.wait_recv()
    wide = 2 * rows
    for j in range(2):
        for zz in range(nz):
            for k in range(taps):
                at = zz * zr + k * mz
                xt[at : at + mz, j * wide : (j + 1) * wide] = fr[j + k, zz * mz : (zz + 1) * mz, :]

    def stem(yk, carry):
        r0 = mo(yk * shard + c * half, 16)
        l0 = mo(yk * half, 16)
        weights = kt[pl.ds(r0, half), :]
        b = biast[pl.ds(r0, half), :]
        for block in range(wide // 128):
            at = block * 128
            values, slopes = [], []
            for j in range(2):
                lanes = pl.ds(j * wide + at, 128)
                v = jnp.dot(weights, xt[:, lanes], preferred_element_type=F32) + b
                phi = 0.5 + 0.5 * lax.erf(v * SQRT_HALF)
                values.append(v * phi)
                slope[pl.ds(l0, half), lanes] = 0.5 * phi + v * (0.5 * INV_SQRT_TWO_PI) * jnp.exp(
                    -0.5 * v * v
                )
            pooled = (0.5 * (values[0] + values[1])).astype(BF16)
            if at < rows:
                pt[pl.ds(r0, half), at : at + 128] = pooled
            else:
                pts[pl.ds(l0, half), at - rows : at - rows + 128] = pooled
        remote(
            pts.at[pl.ds(l0, half)], ptr.at[pl.ds(l0, half)], pt_sem.at[0], pt_sem.at[1], (y, sib)
        ).start()
        return carry

    lax.fori_loop(0, ny, stem, 0)
    own_cot.wait()
    send_cot.wait_recv()
    own_w.wait()

    def back(owners):
        count = len(owners)
        w = jnp.concatenate([wrows(o, 0, half)[...] for o in owners], axis=0)
        gp = lax.dot_general(w, cot2[...], NT, preferred_element_type=F32).astype(BF16).astype(F32)
        for i, o in enumerate(owners):
            l0 = mo(o * half, 16)
            for j in range(2):
                lanes = slice(j * wide, (j + 1) * wide)
                g = gp[i * half : (i + 1) * half] * slope[pl.ds(l0, half), lanes]
                gt[i * lp : i * lp + half, lanes] = g.astype(BF16)
        part = lax.dot_general(
            xt[...], gt[0 : count * lp, :], NT, preferred_element_type=F32
        ).astype(BF16)
        for i, o in enumerate(owners):
            piece = part[:, i * lp : (i + 1) * lp]
            zsend[pl.ds(mo(o * km, 16), km), :] = piece
            own = zsend[pl.ds(mo(o * km + z * zr, 16), zr), :]
            zrecv[pl.ds(mo((o * nz + z) * zr, 16), zr), :] = own

            def pass_on(t, carry):
                zt = lax.rem(z + t, nz)
                remote(
                    zsend.at[pl.ds(mo(o * km + zt * zr, 16), zr)],
                    zrecv.at[pl.ds(mo((o * nz + z) * zr, 16), zr)],
                    z_sem.at[0],
                    z_sem.at[1],
                    (y, zt * nq + q),
                ).start()
                return carry

            lax.fori_loop(1, nz, pass_on, 0)

    back([y])
    for step in range(1, far + 1):
        if step > 1 or far == 1:
            serve(step)
        if step < far:
            back([lax.rem(y + ny - step, ny), lax.rem(y + step, ny)])
        else:
            back([lax.rem(y + far, ny)])

    drain(ptr, pt_sem.at[1])
    drain(wf.at[pl.ds(0, (ny - 1) * half)], sib_recv)
    o0 = 1 - c

    def place_pt(yk, carry):
        pt[pl.ds(mo(yk * shard + o0 * half, 16), half), :] = ptr[pl.ds(mo(yk * half, 16), half), :]
        return carry

    lax.fori_loop(0, ny, place_pt, 0)
    pooled_rows = jnp.transpose(pt[...])
    block_w = 512 if feats % 512 == 0 else feats
    keep = used[:, 0:1] > 0.0

    def project(i, carry):
        lanes = pl.ds(mo(i * block_w, 128), block_w)
        out = jnp.dot(pooled_rows, wf[:, lanes], preferred_element_type=F32) + pbias_ref[:, lanes]
        mscr[:, lanes] = jnp.where(keep, out, 0.0).astype(BF16)
        return carry

    lax.fori_loop(0, feats // block_w, project, 0)
    put = pltpu.make_async_copy(mscr, merged_ref, loc_sem.at[0])
    put.start()

    drain(zrecv.at[pl.ds(0, ny * (nz - 1) * zr)], z_sem.at[1])

    def sum_z(yk, carry):
        acc = jnp.zeros((zr, lp), F32)
        for i in range(nz):
            acc = acc + zrecv[pl.ds(mo((yk * nz + i) * zr, 16), zr), :].astype(F32)
        ysend[pl.ds(mo(yk * zr, 16), zr), :] = acc.astype(BF16)
        return carry

    lax.fori_loop(0, ny, sum_z, 0)
    yrecv[pl.ds(mo(y * zr, 16), zr), :] = ysend[pl.ds(mo(y * zr, 16), zr), :]

    def pass_y(i, carry):
        yt = lax.rem(y + i, ny)
        remote(
            ysend.at[pl.ds(mo(yt * zr, 16), zr)],
            yrecv.at[pl.ds(mo(y * zr, 16), zr)],
            y_sem.at[0],
            y_sem.at[1],
            (yt, s),
        ).start()
        return carry

    lax.fori_loop(1, ny, pass_y, 0)
    drain(yrecv.at[pl.ds(0, (ny - 1) * zr)], y_sem.at[1])
    acc = jnp.zeros((zr, lp), F32)
    for i in range(ny):
        acc = acc + yrecv[i * zr : (i + 1) * zr, :].astype(F32)
    xsend[...] = acc
    xrecv[pl.ds(mo(q * zr, 16), zr), :] = acc

    def pass_x(i, carry):
        remote(
            xsend,
            xrecv.at[pl.ds(mo(q * zr, 16), zr)],
            x_sem.at[0],
            x_sem.at[1],
            (y, z * nq + lax.rem(q + i, nq)),
        ).start()
        return carry

    lax.fori_loop(1, nq, pass_x, 0)
    drain(xrecv.at[pl.ds(0, (nq - 1) * zr)], x_sem.at[1])
    sums = []
    for h in range(NC):
        acc = jnp.zeros((zr, lp), F32)
        for i in range(nx):
            at = (i * NC + h) * zr
            acc = acc + xrecv[at : at + zr, :]
        sums.append(acc)
    line = lax.broadcasted_iota(I32, (zr, lp), 0)
    lane_pad = jnp.zeros((1, lp), F32)
    for m in range(mper):
        for k in range(taps):
            hit = line == k * mz + q * mper + m
            low = jnp.sum(jnp.where(hit, sums[0], 0.0), axis=0, keepdims=True)
            high = jnp.sum(jnp.where(hit, sums[1], 0.0), axis=0, keepdims=True)
            low = jnp.broadcast_to(jnp.concatenate([low, lane_pad], axis=1), (8, 2 * lp))
            high = jnp.broadcast_to(jnp.concatenate([high, lane_pad], axis=1), (8, 2 * lp))
            both = low + pltpu.roll(high, half, 1)
            gw_ref[m, k : k + 1, :] = both[0:1, :shard]

    for way in (0, 1):
        for step in range(1, far + 1):
            ring(step, way).wait_send()
    drain(wf.at[pl.ds(0, (ny - 1) * half)], sib_send)
    drain(posv.at[pl.ds(0, ns - 1)], pos_sem.at[0])
    drain(arr.at[pl.ds(0, (ns - 1) * mr)], msg_sem.at[0])
    send_cot.wait_send()
    send_fr.wait_send()
    drain(pts, pt_sem.at[0])
    drain(zrecv.at[pl.ds(0, ny * (nz - 1) * zr)], z_sem.at[0])
    drain(yrecv.at[pl.ds(0, (ny - 1) * zr)], y_sem.at[0])
    drain(xrecv.at[pl.ds(0, (nq - 1) * zr)], x_sem.at[0])
    put.wait()


def body(nx, mel_frames, positions, conv_weight, conv_bias, proj_weight, proj_bias, cotangent):
    ny, ns = lax.axis_size("dp"), lax.axis_size("seq")
    _, frames, mels = mel_frames.shape
    _, rows, feats = cotangent.shape
    taps, ch = conv_weight.shape[1:]
    tok = frames // 2
    nq = nx * NC
    nz = ns // nq
    km = taps * mels
    zr = km // nz
    half = ch // ny // NC
    lp = -(-half // 128) * 128
    far = ny // 2
    kt = jnp.transpose(conv_weight.reshape(nz, mels // nz, taps, ch), (3, 0, 2, 1)).reshape(ch, km)
    vmem = pl.BlockSpec(memory_space=pltpu.VMEM)
    hbm = pl.BlockSpec(memory_space=pl.ANY)
    total = 4 * rows
    dma = pltpu.SemaphoreType.DMA
    merged, gw = pl.pallas_call(
        functools.partial(kernel, ny, ns, nx),
        out_shape=(
            jax.ShapeDtypeStruct((rows, feats), BF16),
            jax.ShapeDtypeStruct((mels // ns, taps, ch // ny), F32),
        ),
        in_specs=[vmem, vmem, hbm, vmem, hbm, vmem, hbm],
        out_specs=(hbm, vmem),
        scratch_shapes=[
            pltpu.VMEM((ch, feats), BF16),
            pltpu.VMEM((2 * rows, feats), BF16),
            pltpu.VMEM((ch, km), BF16),
            pltpu.VMEM((ch, 128), F32),
            pltpu.VMEM((total, mels), BF16),
            pltpu.VMEM((total, mels), BF16),
            pltpu.VMEM((ns, 1, tok), I32),
            pltpu.VMEM((4, mels, 2 * rows), BF16),
            pltpu.VMEM((km, 4 * rows), BF16),
            pltpu.VMEM((ch, rows), BF16),
            pltpu.VMEM((ch // NC, rows), BF16),
            pltpu.VMEM((ch // NC, rows), BF16),
            pltpu.VMEM((ch // NC, 4 * rows), F32),
            pltpu.VMEM((2 * lp, 4 * rows), BF16),
            pltpu.VMEM((ny * km, lp), BF16),
            pltpu.VMEM((ny * nz * zr, lp), BF16),
            pltpu.VMEM((ny * zr, lp), BF16),
            pltpu.VMEM((ny * zr, lp), BF16),
            pltpu.VMEM((zr, lp), F32),
            pltpu.VMEM((nq * zr, lp), F32),
            pltpu.VMEM((rows, feats), BF16),
            dma((2 * far,)),
            dma((2 * far,)),
            dma,
            dma,
            dma((2,)),
            dma((2,)),
            dma((2,)),
            dma((2,)),
            dma((2,)),
            dma((2,)),
            dma((2,)),
            dma((2,)),
            dma((3,)),
        ],
        compiler_params=pltpu.CompilerParams(
            collective_id=0, has_side_effects=True, vmem_limit_bytes=48 << 20
        ),
    )(
        mel_frames[0],
        positions,
        kt,
        conv_bias[None],
        proj_weight,
        proj_bias[None],
        cotangent[0],
    )
    return (merged[None], gw)


def solution(mesh, nx=NX):
    in_specs = (
        P("dp", "seq", None),
        P("dp", "seq"),
        P(),
        P(),
        P("dp", None),
        P(),
        P("dp", "seq", None),
    )
    out_specs = (P("dp", "seq", None), P("seq", None, "dp"))
    return jax.shard_map(
        functools.partial(body, nx), mesh=mesh, in_specs=in_specs, out_specs=out_specs, check_vma=False
    )
```

```python
import functools

import jax
import jax.numpy as jnp
from jax import lax
from jax.experimental import pallas as pl
from jax.experimental.pallas import tpu as pltpu
from jax.sharding import PartitionSpec as P

SQRT_HALF = 0.7071067811865476
INV_SQRT_TWO_PI = 0.3989422804014327
F32, BF16, I32 = jnp.float32, jnp.bfloat16, jnp.int32
MESH = pl.DeviceIdType.MESH
NT = (((1,), (1,)), ((), ()))
NX, NC = 4, 2


def mo(value, k):
    return pl.multiple_of(value, k)


def steps_of(ny):
    return {8: [[0, 1], [2], [3, 4]], 4: [[0, 1], [2]], 2: [[0], [1]]}[ny]


def groups(ny):
    far = ny // 2
    return [
        [o for t in steps for o in ([t] if t in (0, far) else [t, -t])] for steps in steps_of(ny)
    ]


def kernel(
    ny,
    ns,
    nx,
    mel_ref,
    pos_ref,
    cw_ref,
    bias_ref,
    w_ref,
    pbias_ref,
    cot_ref,
    merged_ref,
    gw_ref,
    wf,
    cot2,
    kt,
    biast,
    msgs,
    arr,
    posv,
    fr,
    xt,
    pt,
    pts,
    ptr,
    slope,
    gt,
    xsend,
    xrecv,
    zsend,
    zrecv,
    ysend,
    yrecv,
    mscr,
    ring_send,
    ring_recv,
    sib_send,
    sib_recv,
    pos_sem,
    msg_sem,
    cot_sem,
    fr_sem,
    pt_sem,
    x_send,
    x_sem,
    z_send,
    z_sem,
    y_sem,
    loc_sem,
):
    nq = nx * NC
    nz = ns // nq
    frames, mels = mel_ref.shape
    tok = frames // 2
    rows = cot_ref.shape[0]
    feats = wf.shape[1]
    ch = wf.shape[0]
    shard = ch // ny
    half = shard // NC
    lanes_g = gt.shape[0]
    cap = rows // ns
    mr = 4 * cap
    km = kt.shape[1]
    taps = km // mels
    mper = mels // ns
    mc = NC * mper
    xr = km // nx
    mx = mels // nx
    zr = taps * mc
    zp = zrecv.shape[0] // (len(groups(ny)) * nz)

    y = lax.axis_index("dp")
    s = lax.axis_index("seq")
    c = lax.rem(s, NC)
    q = lax.rem(s, nq)
    z = s // nq
    x = q // NC
    sib = s + 1 - 2 * c
    up, down = lax.rem(y + 1, ny), lax.rem(y + ny - 1, ny)

    def remote(src, dst, ssem, rsem, dev):
        return pltpu.make_async_remote_copy(
            src_ref=src, dst_ref=dst, send_sem=ssem, recv_sem=rsem, device_id=dev, device_id_type=MESH
        )

    def drain(ref, sem):
        pltpu.make_async_copy(ref, ref, sem).wait()

    barrier = pltpu.get_barrier_semaphore()

    def hail_seq(i, carry):
        pl.semaphore_signal(barrier, inc=1, device_id=(y, lax.rem(s + i, ns)), device_id_type=MESH)
        return carry

    def hail_dp(i, carry):
        yt = lax.rem(y + i, ny)
        pl.semaphore_signal(barrier, inc=1, device_id=(yt, s), device_id_type=MESH)
        pl.semaphore_signal(barrier, inc=1, device_id=(yt, sib), device_id_type=MESH)
        return carry

    lax.fori_loop(1, ny, hail_dp, 0)
    lax.fori_loop(1, ns, hail_seq, 0)

    own_w = pltpu.make_async_copy(w_ref, wf.at[pl.ds(mo(y * shard, 16), shard)], loc_sem.at[0])
    own_w.start()
    own_cot = pltpu.make_async_copy(cot_ref, cot2.at[pl.ds(0, rows)], loc_sem.at[1])
    own_cot.start()

    before = (
        lax.broadcasted_iota(I32, (tok, tok), 0) < lax.broadcasted_iota(I32, (tok, tok), 1)
    ).astype(BF16)
    total = ns * mr

    def spread(hit, value):
        hit_b = hit.astype(F32).astype(BF16)
        rank = jnp.dot(hit_b, before, preferred_element_type=F32)
        lane = lax.broadcasted_iota(I32, (ns, 128), 1)
        table = jnp.zeros((ns, 128), F32)
        for k in range(cap):
            entry = jnp.sum(jnp.where(hit & (rank == k), value + 1.0, 0.0), axis=1, keepdims=True)
            table = table + jnp.where(lane == k, entry, 0.0)
        group = lax.broadcasted_iota(I32, (total, ns), 0) // mr
        expand = (group == lax.broadcasted_iota(I32, (total, ns), 1)).astype(F32).astype(BF16)
        wide = jnp.dot(expand, table.astype(BF16), preferred_element_type=F32)
        n = lax.broadcasted_iota(I32, (total, 128), 0)
        chosen = lax.broadcasted_iota(I32, (total, 128), 1) == lax.rem(n // 4, cap)
        return jnp.sum(jnp.where(chosen, wide, 0.0), axis=1, keepdims=True)

    pos_row = jnp.broadcast_to(pos_ref[...], (ns, tok))
    to_dest = (pos_row // rows) == lax.broadcasted_iota(I32, (ns, tok), 0)
    token = spread(to_dest, lax.broadcasted_iota(I32, (ns, tok), 1).astype(F32))
    n_col = lax.broadcasted_iota(I32, (total, 1), 0)
    f_col = lax.rem(n_col, 4).astype(F32)
    frame = jnp.where(token > 0.0, 2.0 * (token - 1.0) - 1.0 + f_col, -100.0)
    pick = (lax.broadcasted_iota(I32, (total, frames), 1).astype(F32) == frame).astype(F32)
    p = lax.broadcasted_iota(I32, (mels, mels), 1)
    from_m = lax.rem(p // mc, nz) * (nx * mc) + (p // mx) * mc + lax.rem(p, mc)
    order = (lax.broadcasted_iota(I32, (mels, mels), 0) == from_m).astype(F32).astype(BF16)
    mel_p = jnp.dot(mel_ref[...], order, preferred_element_type=F32).astype(BF16)
    msgs[...] = jnp.dot(pick.astype(BF16), mel_p, preferred_element_type=F32).astype(BF16)
    own_slot = pl.ds(mo(s * mr, 16), mr)
    arr[own_slot, :] = msgs[own_slot, :]
    posv[s] = pos_ref[...]

    for k in range(taps):
        turned = jnp.transpose(cw_ref[k * mels : (k + 1) * mels, :])
        kt[:, k * mels : (k + 1) * mels] = jnp.dot(
            turned, order, preferred_element_type=F32
        ).astype(BF16)
    for i in range(ch // 128):
        block = jnp.broadcast_to(bias_ref[128 * i : 128 * (i + 1)][None, :], (128, 128))
        biast[128 * i : 128 * (i + 1), :] = jnp.transpose(block)
    gt[...] = jnp.zeros_like(gt)

    pl.semaphore_wait(barrier, 2 * (ny - 1) + ns - 1)

    far = ny // 2
    cut = -(-(half // 2) // 16) * 16

    def wrows(owner, lo, size):
        return wf.at[pl.ds(mo(owner * shard + c * half + lo, 16), size)]

    def ring(step, way):
        owner = lax.rem(y + ny + 1 - step if way == 0 else y + step - 1, ny)
        if step < far:
            lo, size = 0, half
        else:
            lo, size = (0, cut) if way == 0 else (cut, half - cut)
        if step == 1:
            src = w_ref.at[pl.ds(mo(c * half + lo, 16), size)]
        else:
            src = wrows(owner, lo, size)
        target = (up, s) if way == 0 else (down, s)
        i = way * far + step - 1
        return remote(src, wrows(owner, lo, size), ring_send.at[i], ring_recv.at[i], target)

    def came(step, way):
        owner = lax.rem(y + ny - step if way == 0 else y + step, ny)
        if step < far:
            lo, size = 0, half
        else:
            lo, size = (0, cut) if way == 0 else (cut, half - cut)
        return wrows(owner, lo, size)

    def to_sibling(step, way):
        part = came(step, way)
        return remote(part, part, sib_send, sib_recv, (y, sib))

    def serve(step):
        for way in (0, 1):
            part = came(step, way)
            pltpu.make_async_copy(part, part, ring_recv.at[way * far + step - 1]).wait()
            if step < far:
                ring(step + 1, way).start()
            to_sibling(step, way).start()

    ring(1, 0).start()
    ring(1, 1).start()

    def post(i, carry):
        hop = (i + 1) // 2
        to = lax.rem(s + ns + hop * (2 * lax.rem(i, 2) - 1), ns)
        remote(posv.at[s], posv.at[s], pos_sem.at[0], pos_sem.at[1], (y, to)).start()
        remote(
            msgs.at[pl.ds(mo(to * mr, 16), mr)],
            arr.at[pl.ds(mo(s * mr, 16), mr)],
            msg_sem.at[0],
            msg_sem.at[1],
            (y, to),
        ).start()
        return carry

    lax.fori_loop(1, ns, post, 0)
    send_cot = remote(
        cot_ref, cot2.at[pl.ds(rows, rows)], cot_sem.at[0], cot_sem.at[1], (y, sib)
    )
    send_cot.start()

    drain(posv.at[pl.ds(0, ns - 1)], pos_sem.at[1])
    all_pos = jnp.reshape(posv[...], (ns, tok))
    mine = (all_pos // rows) == s
    slot_row = spread(mine, lax.rem(all_pos, rows).astype(F32)) - 1.0
    row_lane = lax.broadcasted_iota(I32, (total, rows), 1).astype(F32)
    at_row = row_lane == slot_row
    n_f = lax.rem(lax.broadcasted_iota(I32, (total, rows), 0), 4)
    places = [(at_row & (n_f == f)).astype(F32).astype(BF16) for f in range(4)]
    used = lax.dot_general(
        places[0], jnp.ones((total, 128), BF16), (((0,), (0,)), ((), ())), preferred_element_type=F32
    )
    drain(arr.at[pl.ds(0, (ns - 1) * mr)], msg_sem.at[1])
    arr_t = jnp.transpose(arr[...])
    for f in range(4):
        fr[f * mels : (f + 1) * mels, 0:rows] = jnp.dot(arr_t, places[f], preferred_element_type=F32).astype(BF16)
    send_fr = remote(
        fr.at[:, pl.ds(0, rows)], fr.at[:, pl.ds(rows, rows)], fr_sem.at[0], fr_sem.at[1], (y, sib)
    )
    send_fr.start()
    if far > 1:
        serve(1)
    send_fr.wait_recv()
    wide = 2 * rows
    for j in range(2):
        for xx in range(nx):
            for k in range(taps):
                at = xx * xr + k * mx
                xt[at : at + mx, j * wide : (j + 1) * wide] = fr[
                    (j + k) * mels + xx * mx : (j + k) * mels + (xx + 1) * mx, :
                ]

    def stem(yk, carry):
        r0 = mo(yk * shard + c * half, 16)
        l0 = mo(yk * half, 16)
        weights = kt[pl.ds(r0, half), :]
        b = biast[pl.ds(r0, half), :]
        for block in range(wide // 128):
            at = block * 128
            values, slopes = [], []
            for j in range(2):
                lanes = pl.ds(j * wide + at, 128)
                window = fr[j * mels : j * mels + km, at : at + 128]
                v = jnp.dot(weights, window, preferred_element_type=F32) + b
                phi = 0.5 + 0.5 * lax.erf(v * SQRT_HALF)
                values.append(v * phi)
                slope[pl.ds(l0, half), lanes] = 0.5 * phi + v * (0.5 * INV_SQRT_TWO_PI) * jnp.exp(
                    -0.5 * v * v
                )
            pooled = (0.5 * (values[0] + values[1])).astype(BF16)
            if at < rows:
                pt[pl.ds(r0, half), at : at + 128] = pooled
            else:
                pts[pl.ds(l0, half), at - rows : at - rows + 128] = pooled
        remote(
            pts.at[pl.ds(l0, half)], ptr.at[pl.ds(l0, half)], pt_sem.at[0], pt_sem.at[1], (y, sib)
        ).start()
        return carry

    lax.fori_loop(0, ny, stem, 0)
    own_cot.wait()
    send_cot.wait_recv()
    own_w.wait()

    def shard_at(offset):
        return lax.rem(y + ny + offset, ny)

    def back(g):
        offsets = groups(ny)[g]
        w = jnp.concatenate([wrows(shard_at(o), 0, half)[...] for o in offsets], axis=0)
        gp = lax.dot_general(w, cot2[...], NT, preferred_element_type=F32).astype(BF16).astype(F32)
        for i, o in enumerate(offsets):
            l0 = mo(shard_at(o) * half, 16)
            for j in range(2):
                lanes = slice(j * wide, (j + 1) * wide)
                grad = gp[i * half : (i + 1) * half] * slope[pl.ds(l0, half), lanes]
                gt[i * half : (i + 1) * half, lanes] = grad.astype(BF16)
        part = lax.dot_general(xt[...], gt[...], NT, preferred_element_type=F32)
        xsend[g * km : (g + 1) * km, :] = part.astype(BF16)
        mine_x = pl.ds(mo((g * nx + x) * xr, 16), xr)
        xrecv[mine_x, :] = xsend[pl.ds(mo(g * km + x * xr, 16), xr), :]

        def pass_x(t, carry):
            to = lax.rem(x + t, nx)
            remote(
                xsend.at[pl.ds(mo(g * km + to * xr, 16), xr)],
                xrecv.at[mine_x],
                x_send.at[g],
                x_sem.at[g],
                (y, z * nq + to * NC + c),
            ).start()
            return carry

        lax.fori_loop(1, nx, pass_x, 0)

    n_new = lax.broadcasted_iota(I32, (nz * zp, xr), 0)
    in_z = lax.rem(n_new, zp)
    old = (in_z // mc) * mx + (n_new // zp) * mc + lax.rem(in_z, mc)
    regroup = (
        ((lax.broadcasted_iota(I32, (nz * zp, xr), 1) == old) & (in_z < zr)).astype(F32).astype(BF16)
    )

    def middle(g):
        if nx > 1:
            drain(xrecv.at[pl.ds(0, (nx - 1) * xr)], x_sem.at[g])
        acc = jnp.zeros((xr, lanes_g), F32)
        for i in range(nx):
            acc = acc + xrecv[(g * nx + i) * xr : (g * nx + i + 1) * xr, :].astype(F32)
        zsend[g * nz * zp : (g + 1) * nz * zp, :] = jnp.dot(
            regroup, acc.astype(BF16), preferred_element_type=F32
        ).astype(BF16)
        mine_z = pl.ds(mo((g * nz + z) * zp, 16), zp)
        zrecv[mine_z, :] = zsend[mine_z, :]

        def pass_z(t, carry):
            hop = (t + 1) // 2
            to = lax.rem(z + nz + hop * (2 * lax.rem(t, 2) - 1), nz)
            remote(
                zsend.at[pl.ds(mo((g * nz + to) * zp, 16), zp)],
                zrecv.at[mine_z],
                z_send.at[g],
                z_sem.at[g],
                (y, to * nq + q),
            ).start()
            return carry

        lax.fori_loop(1, nz, pass_z, 0)

    def last(g):
        if nz > 1:
            drain(zrecv.at[pl.ds(0, (nz - 1) * zp)], z_sem.at[g])
        acc = jnp.zeros((zp, lanes_g), F32)
        for i in range(nz):
            acc = acc + zrecv[(g * nz + i) * zp : (g * nz + i + 1) * zp, :].astype(F32)
        for i, o in enumerate(groups(ny)[g]):
            turned = pltpu.roll(acc, lanes_g - i * half, 1) if i else acc
            slot = (sum(len(h) for h in groups(ny)[:g]) + i) * zp
            ysend[slot : slot + zp, :] = turned[:, : ysend.shape[1]].astype(BF16)
            here = yrecv.at[pl.ds(mo((y * NC + c) * zp, 16), zp)]
            piece = ysend.at[pl.ds(slot, zp)]
            to = shard_at(o)
            if o == 0:
                yrecv[pl.ds(mo((y * NC + c) * zp, 16), zp), :] = ysend[slot : slot + zp, :]
            else:
                remote(piece, here, y_sem.at[0], y_sem.at[1], (to, s)).start()
            remote(piece, here, y_sem.at[0], y_sem.at[1], (to, sib)).start()

    for g, steps in enumerate(steps_of(ny)):
        for step in steps:
            if step > 1 or (step == 1 and far == 1):
                serve(step)
        back(g)
        if g > 0:
            middle(g - 1)

    drain(ptr, pt_sem.at[1])
    drain(wf.at[pl.ds(0, (ny - 1) * half)], sib_recv)
    o0 = 1 - c

    def place_pt(yk, carry):
        pt[pl.ds(mo(yk * shard + o0 * half, 16), half), :] = ptr[pl.ds(mo(yk * half, 16), half), :]
        return carry

    lax.fori_loop(0, ny, place_pt, 0)
    pooled_rows = jnp.transpose(pt[...])
    block_w = 512 if feats % 512 == 0 else feats
    keep = used[:, 0:1] > 0.0

    def project(i, carry):
        lanes = pl.ds(mo(i * block_w, 128), block_w)
        out = jnp.dot(pooled_rows, wf[:, lanes], preferred_element_type=F32) + pbias_ref[:, lanes]
        mscr[:, lanes] = jnp.where(keep, out, 0.0).astype(BF16)
        return carry

    lax.fori_loop(0, feats // block_w, project, 0)
    put = pltpu.make_async_copy(mscr, merged_ref, loc_sem.at[0])
    put.start()

    middle(len(groups(ny)) - 1)
    for g in range(len(groups(ny))):
        last(g)
    drain(yrecv.at[pl.ds(0, (ny * NC - 1) * zp)], y_sem.at[1])
    sums = []
    for h in range(NC):
        acc = jnp.zeros((zp, yrecv.shape[1]), F32)
        for i in range(ny):
            at = (i * NC + h) * zp
            acc = acc + yrecv[at : at + zp, :].astype(F32)
        pad = jnp.zeros((zp, lanes_g - acc.shape[1]), F32)
        acc = jnp.concatenate([acc, pad], axis=1) if pad.shape[1] else acc
        lane = lax.broadcasted_iota(I32, acc.shape, 1)
        sums.append(jnp.where(lane < half, acc, 0.0))
    both = sums[0] + pltpu.roll(sums[1], half, 1)
    line = lax.broadcasted_iota(I32, both.shape, 0)
    for m in range(mper):
        for k in range(taps):
            hit = line == k * mc + c * mper + m
            one = jnp.sum(jnp.where(hit, both, 0.0), axis=0, keepdims=True)
            gw_ref[k, m : m + 1, :] = one[:, :shard]

    for way in (0, 1):
        for step in range(1, far + 1):
            ring(step, way).wait_send()
    drain(wf.at[pl.ds(0, (ny - 1) * half)], sib_send)
    drain(posv.at[pl.ds(0, ns - 1)], pos_sem.at[0])
    drain(arr.at[pl.ds(0, (ns - 1) * mr)], msg_sem.at[0])
    send_cot.wait_send()
    send_fr.wait_send()
    drain(pts, pt_sem.at[0])
    for g in range(len(groups(ny))):
        if nx > 1:
            drain(xrecv.at[pl.ds(0, (nx - 1) * xr)], x_send.at[g])
        if nz > 1:
            drain(zrecv.at[pl.ds(0, (nz - 1) * zp)], z_send.at[g])
    drain(yrecv.at[pl.ds(0, (ny * NC - 1) * zp)], y_sem.at[0])
    put.wait()


def body(nx, mel_frames, positions, conv_weight, conv_bias, proj_weight, proj_bias, cotangent):
    ny, ns = lax.axis_size("dp"), lax.axis_size("seq")
    _, frames, mels = mel_frames.shape
    _, rows, feats = cotangent.shape
    taps, ch = conv_weight.shape[1:]
    tok = frames // 2
    nq = nx * NC
    nz = ns // nq
    km = taps * mels
    half = ch // ny // NC
    far = ny // 2
    n_groups = len(groups(ny))
    lanes_g = -(-max(max(len(g) for g in groups(ny)) * half, ch // ny) // 128) * 128
    lanes_y = -(-half // 128) * 128
    xr = km // nx
    zp = -(-taps * NC * (mels // ns) // 16) * 16
    cw = jnp.transpose(conv_weight, (1, 0, 2)).reshape(km, ch)
    vmem = pl.BlockSpec(memory_space=pltpu.VMEM)
    hbm = pl.BlockSpec(memory_space=pl.ANY)
    total = 4 * rows
    dma = pltpu.SemaphoreType.DMA
    merged, gw = pl.pallas_call(
        functools.partial(kernel, ny, ns, nx),
        out_shape=(
            jax.ShapeDtypeStruct((rows, feats), BF16),
            jax.ShapeDtypeStruct((taps, mels // ns, ch // ny), F32),
        ),
        in_specs=[vmem, vmem, vmem, vmem, hbm, vmem, hbm],
        out_specs=(hbm, vmem),
        scratch_shapes=[
            pltpu.VMEM((ch, feats), BF16),
            pltpu.VMEM((2 * rows, feats), BF16),
            pltpu.VMEM((ch, km), BF16),
            pltpu.VMEM((ch, 128), F32),
            pltpu.VMEM((total, mels), BF16),
            pltpu.VMEM((total, mels), BF16),
            pltpu.VMEM((ns, 1, tok), I32),
            pltpu.VMEM((4 * mels, 2 * rows), BF16),
            pltpu.VMEM((km, 4 * rows), BF16),
            pltpu.VMEM((ch, rows), BF16),
            pltpu.VMEM((ch // NC, rows), BF16),
            pltpu.VMEM((ch // NC, rows), BF16),
            pltpu.VMEM((ch // NC, 4 * rows), F32),
            pltpu.VMEM((lanes_g, 4 * rows), BF16),
            pltpu.VMEM((n_groups * km, lanes_g), BF16),
            pltpu.VMEM((n_groups * km, lanes_g), BF16),
            pltpu.VMEM((n_groups * nz * zp, lanes_g), BF16),
            pltpu.VMEM((n_groups * nz * zp, lanes_g), BF16),
            pltpu.VMEM((ny * zp, lanes_y), BF16),
            pltpu.VMEM((ny * NC * zp, lanes_y), BF16),
            pltpu.VMEM((rows, feats), BF16),
            dma((2 * far,)),
            dma((2 * far,)),
            dma,
            dma,
            dma((2,)),
            dma((2,)),
            dma((2,)),
            dma((2,)),
            dma((2,)),
            dma((n_groups,)),
            dma((n_groups,)),
            dma((n_groups,)),
            dma((n_groups,)),
            dma((2,)),
            dma((2,)),
        ],
        compiler_params=pltpu.CompilerParams(
            collective_id=0, has_side_effects=True, vmem_limit_bytes=48 << 20
        ),
    )(
        mel_frames[0],
        positions,
        cw,
        conv_bias,
        proj_weight,
        proj_bias[None],
        cotangent[0],
    )
    return (merged[None], jnp.transpose(gw, (1, 0, 2)))


def solution(mesh, nx=NX):
    in_specs = (
        P("dp", "seq", None),
        P("dp", "seq"),
        P(),
        P(),
        P("dp", None),
        P(),
        P("dp", "seq", None),
    )
    out_specs = (P("dp", "seq", None), P("seq", None, "dp"))
    return jax.shard_map(
        functools.partial(body, nx), mesh=mesh, in_specs=in_specs, out_specs=out_specs, check_vma=False
    )
```

```python
import functools

import jax
import jax.numpy as jnp
from jax import lax
from jax.experimental import pallas as pl
from jax.experimental.pallas import tpu as pltpu
from jax.sharding import PartitionSpec as P

SQRT_HALF = 0.7071067811865476
INV_SQRT_TWO_PI = 0.3989422804014327
F32, BF16, I32 = jnp.float32, jnp.bfloat16, jnp.int32
MESH = pl.DeviceIdType.MESH
NT = (((1,), (1,)), ((), ()))
NX, NC = 4, 2


def mo(value, k):
    return pl.multiple_of(value, k)


def steps_of(ny):
    return {8: [[0, 1], [2], [3, 4]], 4: [[0, 1], [2]], 2: [[0], [1]]}[ny]


def groups(ny):
    far = ny // 2
    return [
        [o for t in steps for o in ([t] if t in (0, far) else [t, -t])] for steps in steps_of(ny)
    ]


def kernel(
    ny,
    ns,
    nx,
    mel_in,
    pos_in,
    cw_in,
    bias_in,
    w_ref,
    pbias_in,
    cot_ref,
    merged_ref,
    gw_ref,
    mel_ref,
    pos_ref,
    cw_ref,
    bias_ref,
    pbias_ref,
    wf,
    cot2,
    kt,
    biast,
    msgs,
    arr,
    posv,
    fr,
    xt,
    pt,
    pts,
    ptr,
    slope,
    gt,
    xsend,
    xrecv,
    zsend,
    zrecv,
    ysend,
    yrecv,
    mscr,
    ring_send,
    ring_recv,
    sib_send,
    sib_recv,
    share_send,
    share_recv,
    pos_sem,
    msg_sem,
    cot_sem,
    fr_sem,
    pt_sem,
    x_send,
    x_sem,
    z_send,
    z_sem,
    y_sem,
    loc_sem,
):
    nq = nx * NC
    nz = ns // nq
    frames, mels = mel_ref.shape
    tok = frames // 2
    rows = cot_ref.shape[0]
    feats = wf.shape[1]
    ch = wf.shape[0]
    shard = ch // ny
    half = shard // NC
    lanes_g = gt.shape[0]
    cap = rows // ns
    mr = 4 * cap
    km = kt.shape[1]
    taps = km // mels
    mper = mels // ns
    mc = NC * mper
    xr = km // nx
    mx = mels // nx
    zr = taps * mc
    zp = zrecv.shape[0] // (len(groups(ny)) * nz)

    y = lax.axis_index("dp")
    s = lax.axis_index("seq")
    c = lax.rem(s, NC)
    q = lax.rem(s, nq)
    z = s // nq
    x = q // NC
    sib = s + 1 - 2 * c
    up, down = lax.rem(y + 1, ny), lax.rem(y + ny - 1, ny)

    def remote(src, dst, ssem, rsem, dev):
        return pltpu.make_async_remote_copy(
            src_ref=src, dst_ref=dst, send_sem=ssem, recv_sem=rsem, device_id=dev, device_id_type=MESH
        )

    def drain(ref, sem):
        pltpu.make_async_copy(ref, ref, sem).wait()

    barrier = pltpu.get_barrier_semaphore()

    def hail_seq(i, carry):
        pl.semaphore_signal(barrier, inc=1, device_id=(y, lax.rem(s + i, ns)), device_id_type=MESH)
        return carry

    def hail_dp(i, carry):
        yt = lax.rem(y + i, ny)
        pl.semaphore_signal(barrier, inc=1, device_id=(yt, s), device_id_type=MESH)
        pl.semaphore_signal(barrier, inc=1, device_id=(yt, sib), device_id_type=MESH)
        return carry

    lax.fori_loop(1, ny, hail_dp, 0)
    lax.fori_loop(1, ns, hail_seq, 0)

    own_w = pltpu.make_async_copy(w_ref, wf.at[pl.ds(mo(y * shard, 16), shard)], loc_sem.at[0])
    own_cot = pltpu.make_async_copy(cot_ref, cot2.at[pl.ds(0, rows)], loc_sem.at[1])
    loads = [
        pltpu.make_async_copy(src, dst, loc_sem.at[2 + i])
        for i, (src, dst) in enumerate(
            [
                (pos_in, pos_ref),
                (mel_in, mel_ref),
                (cw_in, cw_ref),
                (bias_in, bias_ref),
                (pbias_in, pbias_ref),
            ]
        )
    ]
    for load in loads:
        load.start()
    own_w.start()
    own_cot.start()
    loads[0].wait()
    loads[1].wait()

    before = (
        lax.broadcasted_iota(I32, (tok, tok), 0) < lax.broadcasted_iota(I32, (tok, tok), 1)
    ).astype(BF16)
    total = ns * mr

    def spread(hit, value):
        hit_b = hit.astype(F32).astype(BF16)
        rank = jnp.dot(hit_b, before, preferred_element_type=F32)
        lane = lax.broadcasted_iota(I32, (ns, 128), 1)
        table = jnp.zeros((ns, 128), F32)
        for k in range(cap):
            entry = jnp.sum(jnp.where(hit & (rank == k), value + 1.0, 0.0), axis=1, keepdims=True)
            table = table + jnp.where(lane == k, entry, 0.0)
        group = lax.broadcasted_iota(I32, (total, ns), 0) // mr
        expand = (group == lax.broadcasted_iota(I32, (total, ns), 1)).astype(F32).astype(BF16)
        wide = jnp.dot(expand, table.astype(BF16), preferred_element_type=F32)
        n = lax.broadcasted_iota(I32, (total, 128), 0)
        chosen = lax.broadcasted_iota(I32, (total, 128), 1) == lax.rem(n // 4, cap)
        return jnp.sum(jnp.where(chosen, wide, 0.0), axis=1, keepdims=True)

    pos_row = jnp.broadcast_to(pos_ref[...], (ns, tok))
    to_dest = (pos_row // rows) == lax.broadcasted_iota(I32, (ns, tok), 0)
    token = spread(to_dest, lax.broadcasted_iota(I32, (ns, tok), 1).astype(F32))
    n_col = lax.broadcasted_iota(I32, (total, 1), 0)
    f_col = lax.rem(n_col, 4).astype(F32)
    frame = jnp.where(token > 0.0, 2.0 * (token - 1.0) - 1.0 + f_col, -100.0)
    pick = (lax.broadcasted_iota(I32, (total, frames), 1).astype(F32) == frame).astype(F32)
    p = lax.broadcasted_iota(I32, (mels, mels), 1)
    from_m = lax.rem(p // mc, nz) * (nx * mc) + (p // mx) * mc + lax.rem(p, mc)
    order = (lax.broadcasted_iota(I32, (mels, mels), 0) == from_m).astype(F32).astype(BF16)
    mel_p = jnp.dot(mel_ref[...], order, preferred_element_type=F32).astype(BF16)
    msgs[...] = jnp.dot(pick.astype(BF16), mel_p, preferred_element_type=F32).astype(BF16)
    own_slot = pl.ds(mo(s * mr, 16), mr)
    arr[own_slot, :] = msgs[own_slot, :]
    posv[s] = pos_ref[...]

    for load in loads[2:]:
        load.wait()
    for k in range(taps):
        turned = jnp.transpose(cw_ref[k * mels : (k + 1) * mels, :])
        kt[:, k * mels : (k + 1) * mels] = jnp.dot(
            turned, order, preferred_element_type=F32
        ).astype(BF16)
    for i in range(ch // 128):
        block = jnp.broadcast_to(bias_ref[128 * i : 128 * (i + 1)][None, :], (128, 128))
        biast[128 * i : 128 * (i + 1), :] = jnp.transpose(block)
    gt[...] = jnp.zeros_like(gt)

    own_w.wait()
    pl.semaphore_wait(barrier, 2 * (ny - 1) + ns - 1)

    far = ny // 2
    cut = -(-(half // 2) // 16) * 16

    shared = feats // 2
    part = shared // nx

    def wrows(owner, lo, size):
        return wf.at[pl.ds(mo(owner * shard + c * half + lo, 16), size)]

    def span(step, way):
        if step < far:
            return 0, half
        return (0, cut) if way == 0 else (cut, half - cut)

    def piece(owner, step, way, kind):
        lo, size = span(step, way)
        row = pl.ds(mo(owner * shard + c * half + lo, 16), size)
        if kind == 0:
            return wf.at[row, pl.ds(mo(shared + x * part, 128), part)]
        return wf.at[row, pl.ds(0, shared)]

    def ring_sem(step, way, kind):
        return (way * far + step - 1) * 2 + kind

    def ring(step, way, kind):
        owner = lax.rem(y + ny + 1 - step if way == 0 else y + step - 1, ny)
        ref = piece(owner, step, way, kind)
        i = ring_sem(step, way, kind)
        target = (up, s) if way == 0 else (down, s)
        return remote(ref, ref, ring_send.at[i], ring_recv.at[i], target)

    def source(step, way):
        return lax.rem(y + ny - step if way == 0 else y + step, ny)

    def serve(step, kind):
        for way in (0, 1):
            ref = piece(source(step, way), step, way, kind)
            pltpu.make_async_copy(ref, ref, ring_recv.at[ring_sem(step, way, kind)]).wait()
            if step < far:
                ring(step + 1, way, kind).start()
            if kind == 1:
                remote(ref, ref, sib_send, sib_recv, (y, sib)).start()
            else:
                for t in range(1, nx):
                    to = lax.rem(x + t, nx)
                    remote(
                        ref,
                        ref,
                        share_send,
                        share_recv.at[way * far + step - 1],
                        (y, z * nq + to * NC + c),
                    ).start()

    def gather(step):
        for way in (0, 1):
            lo, size = span(step, way)
            row = pl.ds(mo(source(step, way) * shard + c * half + lo, 16), size)
            if nx > 1:
                drain(wf.at[row, pl.ds(0, (nx - 1) * part)], share_recv.at[way * far + step - 1])
            ref = wf.at[row, pl.ds(shared, shared)]
            remote(ref, ref, sib_send, sib_recv, (y, sib)).start()

    for kind in (0, 1):
        for way in (0, 1):
            ring(1, way, kind).start()

    def post(i, carry):
        hop = (i + 1) // 2
        to = lax.rem(s + ns + hop * (2 * lax.rem(i, 2) - 1), ns)
        remote(posv.at[s], posv.at[s], pos_sem.at[0], pos_sem.at[1], (y, to)).start()
        remote(
            msgs.at[pl.ds(mo(to * mr, 16), mr)],
            arr.at[pl.ds(mo(s * mr, 16), mr)],
            msg_sem.at[0],
            msg_sem.at[1],
            (y, to),
        ).start()
        return carry

    lax.fori_loop(1, ns, post, 0)
    send_cot = remote(
        cot_ref, cot2.at[pl.ds(rows, rows)], cot_sem.at[0], cot_sem.at[1], (y, sib)
    )
    send_cot.start()

    serve(1, 0)
    drain(posv.at[pl.ds(0, ns - 1)], pos_sem.at[1])
    all_pos = jnp.reshape(posv[...], (ns, tok))
    mine = (all_pos // rows) == s
    slot_row = spread(mine, lax.rem(all_pos, rows).astype(F32)) - 1.0
    row_lane = lax.broadcasted_iota(I32, (total, rows), 1).astype(F32)
    at_row = row_lane == slot_row
    n_f = lax.rem(lax.broadcasted_iota(I32, (total, rows), 0), 4)
    places = [(at_row & (n_f == f)).astype(F32).astype(BF16) for f in range(4)]
    used = lax.dot_general(
        places[0], jnp.ones((total, 128), BF16), (((0,), (0,)), ((), ())), preferred_element_type=F32
    )
    serve(1, 1)
    drain(arr.at[pl.ds(0, (ns - 1) * mr)], msg_sem.at[1])
    arr_t = jnp.transpose(arr[...])
    for f in range(4):
        fr[f * mels : (f + 1) * mels, 0:rows] = jnp.dot(arr_t, places[f], preferred_element_type=F32).astype(BF16)
    send_fr = remote(
        fr.at[:, pl.ds(0, rows)], fr.at[:, pl.ds(rows, rows)], fr_sem.at[0], fr_sem.at[1], (y, sib)
    )
    send_fr.start()
    if far > 1:
        serve(2, 0)
    gather(1)
    send_fr.wait_recv()
    wide = 2 * rows
    for j in range(2):
        for xx in range(nx):
            for k in range(taps):
                at = xx * xr + k * mx
                xt[at : at + mx, j * wide : (j + 1) * wide] = fr[
                    (j + k) * mels + xx * mx : (j + k) * mels + (xx + 1) * mx, :
                ]

    def stem(yk, carry):
        r0 = mo(yk * shard + c * half, 16)
        l0 = mo(yk * half, 16)
        weights = kt[pl.ds(r0, half), :]
        b = biast[pl.ds(r0, half), :]
        for block in range(wide // 128):
            at = block * 128
            values, slopes = [], []
            for j in range(2):
                lanes = pl.ds(j * wide + at, 128)
                window = fr[j * mels : j * mels + km, at : at + 128]
                v = jnp.dot(weights, window, preferred_element_type=F32) + b
                phi = 0.5 + 0.5 * lax.erf(v * SQRT_HALF)
                values.append(v * phi)
                slope[pl.ds(l0, half), lanes] = 0.5 * phi + v * (0.5 * INV_SQRT_TWO_PI) * jnp.exp(
                    -0.5 * v * v
                )
            pooled = (0.5 * (values[0] + values[1])).astype(BF16)
            if at < rows:
                pt[pl.ds(r0, half), at : at + 128] = pooled
            else:
                pts[pl.ds(l0, half), at - rows : at - rows + 128] = pooled
        remote(
            pts.at[pl.ds(l0, half)], ptr.at[pl.ds(l0, half)], pt_sem.at[0], pt_sem.at[1], (y, sib)
        ).start()
        return carry

    if far > 1:
        lax.fori_loop(0, ny // 2, stem, 0)
        serve(2, 1)
        lax.fori_loop(ny // 2, ny, stem, 0)
    else:
        lax.fori_loop(0, ny, stem, 0)
    own_cot.wait()
    send_cot.wait_recv()

    def shard_at(offset):
        return lax.rem(y + ny + offset, ny)

    def back(g):
        offsets = groups(ny)[g]
        w = jnp.concatenate([wrows(shard_at(o), 0, half)[...] for o in offsets], axis=0)
        gp = lax.dot_general(w, cot2[...], NT, preferred_element_type=F32).astype(BF16).astype(F32)
        for i, o in enumerate(offsets):
            l0 = mo(shard_at(o) * half, 16)
            for j in range(2):
                lanes = slice(j * wide, (j + 1) * wide)
                grad = gp[i * half : (i + 1) * half] * slope[pl.ds(l0, half), lanes]
                gt[i * half : (i + 1) * half, lanes] = grad.astype(BF16)
        product = lax.dot_general(xt[...], gt[...], NT, preferred_element_type=F32)
        xsend[g * km : (g + 1) * km, :] = product.astype(BF16)
        mine_x = pl.ds(mo((g * nx + x) * xr, 16), xr)
        xrecv[mine_x, :] = xsend[pl.ds(mo(g * km + x * xr, 16), xr), :]

        def pass_x(t, carry):
            to = lax.rem(x + t, nx)
            remote(
                xsend.at[pl.ds(mo(g * km + to * xr, 16), xr)],
                xrecv.at[mine_x],
                x_send.at[g],
                x_sem.at[g],
                (y, z * nq + to * NC + c),
            ).start()
            return carry

        lax.fori_loop(1, nx, pass_x, 0)

    n_new = lax.broadcasted_iota(I32, (nz * zp, xr), 0)
    in_z = lax.rem(n_new, zp)
    old = (in_z // mc) * mx + (n_new // zp) * mc + lax.rem(in_z, mc)
    regroup = (
        ((lax.broadcasted_iota(I32, (nz * zp, xr), 1) == old) & (in_z < zr)).astype(F32).astype(BF16)
    )

    def middle(g):
        if nx > 1:
            drain(xrecv.at[pl.ds(0, (nx - 1) * xr)], x_sem.at[g])
        acc = jnp.zeros((xr, lanes_g), F32)
        for i in range(nx):
            acc = acc + xrecv[(g * nx + i) * xr : (g * nx + i + 1) * xr, :].astype(F32)
        zsend[g * nz * zp : (g + 1) * nz * zp, :] = jnp.dot(
            regroup, acc.astype(BF16), preferred_element_type=F32
        ).astype(BF16)
        mine_z = pl.ds(mo((g * nz + z) * zp, 16), zp)
        zrecv[mine_z, :] = zsend[mine_z, :]

        def pass_z(t, carry):
            hop = (t + 1) // 2
            to = lax.rem(z + nz + hop * (2 * lax.rem(t, 2) - 1), nz)
            remote(
                zsend.at[pl.ds(mo((g * nz + to) * zp, 16), zp)],
                zrecv.at[mine_z],
                z_send.at[g],
                z_sem.at[g],
                (y, to * nq + q),
            ).start()
            return carry

        lax.fori_loop(1, nz, pass_z, 0)

    def last(g):
        if nz > 1:
            drain(zrecv.at[pl.ds(0, (nz - 1) * zp)], z_sem.at[g])
        acc = jnp.zeros((zp, lanes_g), F32)
        for i in range(nz):
            acc = acc + zrecv[(g * nz + i) * zp : (g * nz + i + 1) * zp, :].astype(F32)
        for i, o in enumerate(groups(ny)[g]):
            turned = pltpu.roll(acc, lanes_g - i * half, 1) if i else acc
            slot = (sum(len(h) for h in groups(ny)[:g]) + i) * zp
            ysend[slot : slot + zp, :] = turned[:, : ysend.shape[1]].astype(BF16)
            here = yrecv.at[pl.ds(mo((y * NC + c) * zp, 16), zp)]
            mine_y = ysend.at[pl.ds(slot, zp)]
            to = shard_at(o)
            if o == 0:
                yrecv[pl.ds(mo((y * NC + c) * zp, 16), zp), :] = ysend[slot : slot + zp, :]
            else:
                remote(mine_y, here, y_sem.at[0], y_sem.at[1], (to, s)).start()
            remote(mine_y, here, y_sem.at[0], y_sem.at[1], (to, sib)).start()

    for g, steps in enumerate(steps_of(ny)):
        for step in steps:
            if step > 2:
                serve(step, 0)
                serve(step, 1)
        for step in steps:
            if step > 1:
                gather(step)
        back(g)
        if g > 0:
            middle(g - 1)

    drain(ptr, pt_sem.at[1])
    drain(wf.at[pl.ds(0, (ny - 1) * half)], sib_recv)
    o0 = 1 - c

    def place_pt(yk, carry):
        pt[pl.ds(mo(yk * shard + o0 * half, 16), half), :] = ptr[pl.ds(mo(yk * half, 16), half), :]
        return carry

    lax.fori_loop(0, ny, place_pt, 0)
    pooled_rows = jnp.transpose(pt[...])
    block_w = 512 if feats % 512 == 0 else feats
    keep = used[:, 0:1] > 0.0

    def project(i, carry):
        lanes = pl.ds(mo(i * block_w, 128), block_w)
        out = jnp.dot(pooled_rows, wf[:, lanes], preferred_element_type=F32) + pbias_ref[:, lanes]
        mscr[:, lanes] = jnp.where(keep, out, 0.0).astype(BF16)
        return carry

    lax.fori_loop(0, feats // block_w, project, 0)
    put = pltpu.make_async_copy(mscr, merged_ref, loc_sem.at[0])
    put.start()

    middle(len(groups(ny)) - 1)
    for g in range(len(groups(ny))):
        last(g)
    drain(yrecv.at[pl.ds(0, (ny * NC - 1) * zp)], y_sem.at[1])
    sums = []
    for h in range(NC):
        acc = jnp.zeros((zp, yrecv.shape[1]), F32)
        for i in range(ny):
            at = (i * NC + h) * zp
            acc = acc + yrecv[at : at + zp, :].astype(F32)
        pad = jnp.zeros((zp, lanes_g - acc.shape[1]), F32)
        acc = jnp.concatenate([acc, pad], axis=1) if pad.shape[1] else acc
        lane = lax.broadcasted_iota(I32, acc.shape, 1)
        sums.append(jnp.where(lane < half, acc, 0.0))
    both = sums[0] + pltpu.roll(sums[1], half, 1)
    line = lax.broadcasted_iota(I32, both.shape, 0)
    for m in range(mper):
        for k in range(taps):
            hit = line == k * mc + c * mper + m
            one = jnp.sum(jnp.where(hit, both, 0.0), axis=0, keepdims=True)
            gw_ref[k, m : m + 1, :] = one[:, :shard]

    for way in (0, 1):
        for step in range(1, far + 1):
            for kind in (0, 1):
                ring(step, way, kind).wait_send()
    drain(wf.at[pl.ds(0, (ny - 1) * half)], sib_send)
    if nx > 1:
        drain(wf.at[pl.ds(0, (ny - 1) * half), pl.ds(0, (nx - 1) * part)], share_send)
    drain(posv.at[pl.ds(0, ns - 1)], pos_sem.at[0])
    drain(arr.at[pl.ds(0, (ns - 1) * mr)], msg_sem.at[0])
    send_cot.wait_send()
    send_fr.wait_send()
    drain(pts, pt_sem.at[0])
    for g in range(len(groups(ny))):
        if nx > 1:
            drain(xrecv.at[pl.ds(0, (nx - 1) * xr)], x_send.at[g])
        if nz > 1:
            drain(zrecv.at[pl.ds(0, (nz - 1) * zp)], z_send.at[g])
    drain(yrecv.at[pl.ds(0, (ny * NC - 1) * zp)], y_sem.at[0])
    put.wait()


def body(nx, mel_frames, positions, conv_weight, conv_bias, proj_weight, proj_bias, cotangent):
    ny, ns = lax.axis_size("dp"), lax.axis_size("seq")
    _, frames, mels = mel_frames.shape
    _, rows, feats = cotangent.shape
    taps, ch = conv_weight.shape[1:]
    tok = frames // 2
    nq = nx * NC
    nz = ns // nq
    km = taps * mels
    half = ch // ny // NC
    far = ny // 2
    n_groups = len(groups(ny))
    lanes_g = -(-max(max(len(g) for g in groups(ny)) * half, ch // ny) // 128) * 128
    lanes_y = -(-half // 128) * 128
    xr = km // nx
    zp = -(-taps * NC * (mels // ns) // 16) * 16
    cw = jnp.transpose(conv_weight, (1, 0, 2)).reshape(km, ch)
    vmem = pl.BlockSpec(memory_space=pltpu.VMEM)
    hbm = pl.BlockSpec(memory_space=pltpu.HBM)
    total = 4 * rows
    dma = pltpu.SemaphoreType.DMA
    merged, gw = pl.pallas_call(
        functools.partial(kernel, ny, ns, nx),
        out_shape=(
            jax.ShapeDtypeStruct((rows, feats), BF16),
            jax.ShapeDtypeStruct((taps, mels // ns, ch // ny), F32),
        ),
        in_specs=[hbm] * 7,
        out_specs=(hbm, vmem),
        scratch_shapes=[
            pltpu.VMEM((frames, mels), BF16),
            pltpu.VMEM((1, tok), I32),
            pltpu.VMEM((km, ch), BF16),
            pltpu.VMEM((ch,), F32),
            pltpu.VMEM((1, feats), F32),
            pltpu.VMEM((ch, feats), BF16),
            pltpu.VMEM((2 * rows, feats), BF16),
            pltpu.VMEM((ch, km), BF16),
            pltpu.VMEM((ch, 128), F32),
            pltpu.VMEM((total, mels), BF16),
            pltpu.VMEM((total, mels), BF16),
            pltpu.VMEM((ns, 1, tok), I32),
            pltpu.VMEM((4 * mels, 2 * rows), BF16),
            pltpu.VMEM((km, 4 * rows), BF16),
            pltpu.VMEM((ch, rows), BF16),
            pltpu.VMEM((ch // NC, rows), BF16),
            pltpu.VMEM((ch // NC, rows), BF16),
            pltpu.VMEM((ch // NC, 4 * rows), F32),
            pltpu.VMEM((lanes_g, 4 * rows), BF16),
            pltpu.VMEM((n_groups * km, lanes_g), BF16),
            pltpu.VMEM((n_groups * km, lanes_g), BF16),
            pltpu.VMEM((n_groups * nz * zp, lanes_g), BF16),
            pltpu.VMEM((n_groups * nz * zp, lanes_g), BF16),
            pltpu.VMEM((ny * zp, lanes_y), BF16),
            pltpu.VMEM((ny * NC * zp, lanes_y), BF16),
            pltpu.VMEM((rows, feats), BF16),
            dma((4 * far,)),
            dma((4 * far,)),
            dma,
            dma,
            dma,
            dma((2 * far,)),
            dma((2,)),
            dma((2,)),
            dma((2,)),
            dma((2,)),
            dma((2,)),
            dma((n_groups,)),
            dma((n_groups,)),
            dma((n_groups,)),
            dma((n_groups,)),
            dma((2,)),
            dma((7,)),
        ],
        compiler_params=pltpu.CompilerParams(
            collective_id=0, has_side_effects=True, vmem_limit_bytes=60 << 20
        ),
    )(
        mel_frames[0],
        positions,
        cw,
        conv_bias,
        proj_weight,
        proj_bias[None],
        cotangent[0],
    )
    return (merged[None], jnp.transpose(gw, (1, 0, 2)))


def solution(mesh, nx=NX):
    in_specs = (
        P("dp", "seq", None),
        P("dp", "seq"),
        P(),
        P(),
        P("dp", None),
        P(),
        P("dp", "seq", None),
    )
    out_specs = (P("dp", "seq", None), P("seq", None, "dp"))
    return jax.shard_map(
        functools.partial(body, nx), mesh=mesh, in_specs=in_specs, out_specs=out_specs, check_vma=False
    )
```

```python
import functools

import jax
import jax.numpy as jnp
from jax import lax
from jax.experimental import pallas as pl
from jax.experimental.pallas import tpu as pltpu
from jax.sharding import PartitionSpec as P

SQRT_HALF = 0.7071067811865476
INV_SQRT_TWO_PI = 0.3989422804014327
F32, BF16, I32 = jnp.float32, jnp.bfloat16, jnp.int32
MESH = pl.DeviceIdType.MESH
NT = (((1,), (1,)), ((), ()))
NX, NC = 4, 2


def mo(value, k):
    return pl.multiple_of(value, k)


def steps_of(ny):
    return {8: [[0, 1], [2], [3, 4]], 4: [[0, 1], [2]], 2: [[0], [1]]}[ny]


def groups(ny):
    far = ny // 2
    return [
        [o for t in steps for o in ([t] if t in (0, far) else [t, -t])] for steps in steps_of(ny)
    ]


def kernel(
    ny,
    ns,
    nx,
    mel_in,
    pos_in,
    cw_in,
    bias_in,
    w_ref,
    pbias_in,
    cot_ref,
    merged_ref,
    gw_ref,
    mel_ref,
    pos_ref,
    cw_ref,
    bias_ref,
    pbias_ref,
    wf,
    cot2,
    kt,
    biast,
    msgs,
    arr,
    posv,
    fr,
    xt,
    pt,
    pts,
    ptr,
    slope,
    gt,
    xsend,
    xrecv,
    zsend,
    zrecv,
    ysend,
    yrecv,
    ring_send,
    ring_recv,
    sib_send,
    sib_recv,
    share_send,
    share_recv,
    pos_sem,
    msg_sem,
    cot_sem,
    fr_sem,
    pt_sem,
    x_send,
    x_sem,
    z_send,
    z_sem,
    y_sem,
    loc_sem,
):
    nq = nx * NC
    nz = ns // nq
    frames, mels = mel_ref.shape
    tok = frames // 2
    rows = cot_ref.shape[0]
    feats = wf.shape[1]
    ch = wf.shape[0]
    shard = ch // ny
    half = shard // NC
    lanes_g = gt.shape[0]
    cap = rows // ns
    mr = 4 * cap
    km = kt.shape[1]
    taps = km // mels
    mper = mels // ns
    mc = NC * mper
    xr = km // nx
    mx = mels // nx
    zr = taps * mc
    zp = zrecv.shape[0] // (len(groups(ny)) * nz)

    y = lax.axis_index("dp")
    s = lax.axis_index("seq")
    c = lax.rem(s, NC)
    q = lax.rem(s, nq)
    z = s // nq
    x = q // NC
    sib = s + 1 - 2 * c
    up, down = lax.rem(y + 1, ny), lax.rem(y + ny - 1, ny)

    def remote(src, dst, ssem, rsem, dev):
        return pltpu.make_async_remote_copy(
            src_ref=src, dst_ref=dst, send_sem=ssem, recv_sem=rsem, device_id=dev, device_id_type=MESH
        )

    def drain(ref, sem):
        pltpu.make_async_copy(ref, ref, sem).wait()

    barrier = pltpu.get_barrier_semaphore()

    def hail_seq(i, carry):
        pl.semaphore_signal(barrier, inc=1, device_id=(y, lax.rem(s + i, ns)), device_id_type=MESH)
        return carry

    def hail_dp(i, carry):
        yt = lax.rem(y + i, ny)
        pl.semaphore_signal(barrier, inc=1, device_id=(yt, s), device_id_type=MESH)
        pl.semaphore_signal(barrier, inc=1, device_id=(yt, sib), device_id_type=MESH)
        return carry

    lax.fori_loop(1, ny, hail_dp, 0)
    lax.fori_loop(1, ns, hail_seq, 0)

    own_w = pltpu.make_async_copy(w_ref, wf.at[pl.ds(mo(y * shard, 16), shard)], loc_sem.at[0])
    own_cot = pltpu.make_async_copy(cot_ref, cot2.at[pl.ds(0, rows)], loc_sem.at[1])
    loads = [
        pltpu.make_async_copy(src, dst, loc_sem.at[2 + i])
        for i, (src, dst) in enumerate(
            [
                (pos_in, pos_ref),
                (mel_in, mel_ref),
                (cw_in, cw_ref),
                (bias_in, bias_ref),
                (pbias_in, pbias_ref),
            ]
        )
    ]
    for load in loads:
        load.start()
    own_w.start()
    own_cot.start()
    loads[0].wait()
    loads[1].wait()

    before = (
        lax.broadcasted_iota(I32, (tok, tok), 0) < lax.broadcasted_iota(I32, (tok, tok), 1)
    ).astype(BF16)
    total = ns * mr

    def spread(hit, value):
        hit_b = hit.astype(F32).astype(BF16)
        rank = jnp.dot(hit_b, before, preferred_element_type=F32)
        lane = lax.broadcasted_iota(I32, (ns, 128), 1)
        table = jnp.zeros((ns, 128), F32)
        for k in range(cap):
            entry = jnp.sum(jnp.where(hit & (rank == k), value + 1.0, 0.0), axis=1, keepdims=True)
            table = table + jnp.where(lane == k, entry, 0.0)
        group = lax.broadcasted_iota(I32, (total, ns), 0) // mr
        expand = (group == lax.broadcasted_iota(I32, (total, ns), 1)).astype(F32).astype(BF16)
        wide = jnp.dot(expand, table.astype(BF16), preferred_element_type=F32)
        n = lax.broadcasted_iota(I32, (total, 128), 0)
        chosen = lax.broadcasted_iota(I32, (total, 128), 1) == lax.rem(n // 4, cap)
        return jnp.sum(jnp.where(chosen, wide, 0.0), axis=1, keepdims=True)

    pos_row = jnp.broadcast_to(pos_ref[...], (ns, tok))
    to_dest = (pos_row // rows) == lax.broadcasted_iota(I32, (ns, tok), 0)
    token = spread(to_dest, lax.broadcasted_iota(I32, (ns, tok), 1).astype(F32))
    n_col = lax.broadcasted_iota(I32, (total, 1), 0)
    f_col = lax.rem(n_col, 4).astype(F32)
    frame = jnp.where(token > 0.0, 2.0 * (token - 1.0) - 1.0 + f_col, -100.0)
    pick = (lax.broadcasted_iota(I32, (total, frames), 1).astype(F32) == frame).astype(F32)
    p = lax.broadcasted_iota(I32, (mels, mels), 1)
    from_m = lax.rem(p // mc, nz) * (nx * mc) + (p // mx) * mc + lax.rem(p, mc)
    order = (lax.broadcasted_iota(I32, (mels, mels), 0) == from_m).astype(F32).astype(BF16)
    mel_p = jnp.dot(mel_ref[...], order, preferred_element_type=F32).astype(BF16)
    msgs[...] = jnp.dot(pick.astype(BF16), mel_p, preferred_element_type=F32).astype(BF16)
    own_slot = pl.ds(mo(s * mr, 16), mr)
    arr[own_slot, :] = msgs[own_slot, :]
    posv[s] = pos_ref[...]

    for load in loads[2:]:
        load.wait()
    for k in range(taps):
        turned = jnp.transpose(cw_ref[k * mels : (k + 1) * mels, :])
        kt[:, k * mels : (k + 1) * mels] = jnp.dot(
            turned, order, preferred_element_type=F32
        ).astype(BF16)
    for i in range(ch // 128):
        block = jnp.broadcast_to(bias_ref[128 * i : 128 * (i + 1)][None, :], (128, 128))
        biast[128 * i : 128 * (i + 1), :] = jnp.transpose(block)
    gt[...] = jnp.zeros_like(gt)

    own_w.wait()
    pl.semaphore_wait(barrier, 2 * (ny - 1) + ns - 1)

    far = ny // 2
    cut = -(-(half // 2) // 16) * 16

    shared = feats // 2
    part = shared // nx

    def wrows(owner, lo, size):
        return wf.at[pl.ds(mo(owner * shard + c * half + lo, 16), size)]

    def span(step, way):
        if step < far:
            return 0, half
        return (0, cut) if way == 0 else (cut, half - cut)

    def piece(owner, step, way, kind):
        lo, size = span(step, way)
        row = pl.ds(mo(owner * shard + c * half + lo, 16), size)
        if kind == 0:
            return wf.at[row, pl.ds(mo(shared + x * part, 128), part)]
        return wf.at[row, pl.ds((kind - 1) * (shared // 2), shared // 2)]

    def ring_sem(step, way, kind):
        return (way * far + step - 1) * 3 + kind

    def ring(step, way, kind):
        owner = lax.rem(y + ny + 1 - step if way == 0 else y + step - 1, ny)
        ref = piece(owner, step, way, kind)
        i = ring_sem(step, way, kind)
        target = (up, s) if way == 0 else (down, s)
        return remote(ref, ref, ring_send.at[i], ring_recv.at[i], target)

    def source(step, way):
        return lax.rem(y + ny - step if way == 0 else y + step, ny)

    def serve(step, kind):
        for way in (0, 1):
            ref = piece(source(step, way), step, way, kind)
            pltpu.make_async_copy(ref, ref, ring_recv.at[ring_sem(step, way, kind)]).wait()
            if step < far:
                ring(step + 1, way, kind).start()
            if kind:
                remote(ref, ref, sib_send, sib_recv, (y, sib)).start()
            else:
                for t in range(1, nx):
                    to = lax.rem(x + t, nx)
                    remote(
                        ref,
                        ref,
                        share_send,
                        share_recv.at[way * far + step - 1],
                        (y, z * nq + to * NC + c),
                    ).start()

    def gather(step):
        for way in (0, 1):
            lo, size = span(step, way)
            row = pl.ds(mo(source(step, way) * shard + c * half + lo, 16), size)
            if nx > 1:
                drain(wf.at[row, pl.ds(0, (nx - 1) * part)], share_recv.at[way * far + step - 1])
            ref = wf.at[row, pl.ds(shared, shared)]
            remote(ref, ref, sib_send, sib_recv, (y, sib)).start()

    for kind in (0, 1, 2):
        for way in (0, 1):
            ring(1, way, kind).start()

    def post(i, carry):
        hop = (i + 1) // 2
        to = lax.rem(s + ns + hop * (2 * lax.rem(i, 2) - 1), ns)
        remote(posv.at[s], posv.at[s], pos_sem.at[0], pos_sem.at[1], (y, to)).start()
        remote(
            msgs.at[pl.ds(mo(to * mr, 16), mr)],
            arr.at[pl.ds(mo(s * mr, 16), mr)],
            msg_sem.at[0],
            msg_sem.at[1],
            (y, to),
        ).start()
        return carry

    lax.fori_loop(1, ns, post, 0)
    send_cot = remote(
        cot_ref, cot2.at[pl.ds(rows, rows)], cot_sem.at[0], cot_sem.at[1], (y, sib)
    )
    send_cot.start()

    def serve_if(step, kind):
        if step <= far:
            serve(step, kind)

    serve(1, 0)
    serve(1, 1)
    drain(posv.at[pl.ds(0, ns - 1)], pos_sem.at[1])
    all_pos = jnp.reshape(posv[...], (ns, tok))
    mine = (all_pos // rows) == s
    slot_row = spread(mine, lax.rem(all_pos, rows).astype(F32)) - 1.0
    row_lane = lax.broadcasted_iota(I32, (total, rows), 1).astype(F32)
    at_row = row_lane == slot_row
    n_f = lax.rem(lax.broadcasted_iota(I32, (total, rows), 0), 4)
    places = [(at_row & (n_f == f)).astype(F32).astype(BF16) for f in range(4)]
    used = lax.dot_general(
        places[0], jnp.ones((total, 128), BF16), (((0,), (0,)), ((), ())), preferred_element_type=F32
    )
    serve(1, 2)
    serve_if(2, 0)
    serve_if(2, 1)
    drain(arr.at[pl.ds(0, (ns - 1) * mr)], msg_sem.at[1])
    arr_t = jnp.transpose(arr[...])
    for f in range(4):
        fr[f * mels : (f + 1) * mels, 0:rows] = jnp.dot(arr_t, places[f], preferred_element_type=F32).astype(BF16)
    send_fr = remote(
        fr.at[:, pl.ds(0, rows)], fr.at[:, pl.ds(rows, rows)], fr_sem.at[0], fr_sem.at[1], (y, sib)
    )
    send_fr.start()
    serve_if(2, 2)
    serve_if(3, 0)
    send_fr.wait_recv()
    wide = 2 * rows
    for j in range(2):
        for xx in range(nx):
            for k in range(taps):
                at = xx * xr + k * mx
                xt[at : at + mx, j * wide : (j + 1) * wide] = fr[
                    (j + k) * mels + xx * mx : (j + k) * mels + (xx + 1) * mx, :
                ]

    def stem(yk, carry):
        r0 = mo(yk * shard + c * half, 16)
        l0 = mo(yk * half, 16)
        weights = kt[pl.ds(r0, half), :]
        b = biast[pl.ds(r0, half), :]
        for block in range(wide // 128):
            at = block * 128
            values, slopes = [], []
            for j in range(2):
                lanes = pl.ds(j * wide + at, 128)
                window = fr[j * mels : j * mels + km, at : at + 128]
                v = jnp.dot(weights, window, preferred_element_type=F32) + b
                phi = 0.5 + 0.5 * lax.erf(v * SQRT_HALF)
                values.append(v * phi)
                slope[pl.ds(l0, half), lanes] = 0.5 * phi + v * (0.5 * INV_SQRT_TWO_PI) * jnp.exp(
                    -0.5 * v * v
                )
            pooled = (0.5 * (values[0] + values[1])).astype(BF16)
            if at < rows:
                pt[pl.ds(r0, half), at : at + 128] = pooled
            else:
                pts[pl.ds(l0, half), at - rows : at - rows + 128] = pooled
        remote(
            pts.at[pl.ds(l0, half)], ptr.at[pl.ds(l0, half)], pt_sem.at[0], pt_sem.at[1], (y, sib)
        ).start()
        return carry

    serve_if(3, 1)
    gather(1)
    serve_if(4, 0)
    lax.fori_loop(0, ny // 2, stem, 0)
    serve_if(3, 2)
    if far > 1:
        gather(2)
    lax.fori_loop(ny // 2, ny, stem, 0)
    serve_if(4, 1)
    own_cot.wait()
    send_cot.wait_recv()

    def shard_at(offset):
        return lax.rem(y + ny + offset, ny)

    def back(g):
        offsets = groups(ny)[g]
        w = jnp.concatenate([wrows(shard_at(o), 0, half)[...] for o in offsets], axis=0)
        gp = lax.dot_general(w, cot2[...], NT, preferred_element_type=F32).astype(BF16).astype(F32)
        for i, o in enumerate(offsets):
            l0 = mo(shard_at(o) * half, 16)
            for j in range(2):
                lanes = slice(j * wide, (j + 1) * wide)
                grad = gp[i * half : (i + 1) * half] * slope[pl.ds(l0, half), lanes]
                gt[i * half : (i + 1) * half, lanes] = grad.astype(BF16)
        product = lax.dot_general(xt[...], gt[...], NT, preferred_element_type=F32)
        xsend[g * km : (g + 1) * km, :] = product.astype(BF16)
        mine_x = pl.ds(mo((g * nx + x) * xr, 16), xr)
        xrecv[mine_x, :] = xsend[pl.ds(mo(g * km + x * xr, 16), xr), :]

        def pass_x(t, carry):
            to = lax.rem(x + t, nx)
            remote(
                xsend.at[pl.ds(mo(g * km + to * xr, 16), xr)],
                xrecv.at[mine_x],
                x_send.at[g],
                x_sem.at[g],
                (y, z * nq + to * NC + c),
            ).start()
            return carry

        lax.fori_loop(1, nx, pass_x, 0)

    n_new = lax.broadcasted_iota(I32, (nz * zp, xr), 0)
    in_z = lax.rem(n_new, zp)
    old = (in_z // mc) * mx + (n_new // zp) * mc + lax.rem(in_z, mc)
    regroup = (
        ((lax.broadcasted_iota(I32, (nz * zp, xr), 1) == old) & (in_z < zr)).astype(F32).astype(BF16)
    )

    def middle(g):
        if nx > 1:
            drain(xrecv.at[pl.ds(0, (nx - 1) * xr)], x_sem.at[g])
        acc = jnp.zeros((xr, lanes_g), F32)
        for i in range(nx):
            acc = acc + xrecv[(g * nx + i) * xr : (g * nx + i + 1) * xr, :].astype(F32)
        zsend[g * nz * zp : (g + 1) * nz * zp, :] = jnp.dot(
            regroup, acc.astype(BF16), preferred_element_type=F32
        ).astype(BF16)
        mine_z = pl.ds(mo((g * nz + z) * zp, 16), zp)
        zrecv[mine_z, :] = zsend[mine_z, :]

        def pass_z(t, carry):
            hop = (t + 1) // 2
            to = lax.rem(z + nz + hop * (2 * lax.rem(t, 2) - 1), nz)
            remote(
                zsend.at[pl.ds(mo((g * nz + to) * zp, 16), zp)],
                zrecv.at[mine_z],
                z_send.at[g],
                z_sem.at[g],
                (y, to * nq + q),
            ).start()
            return carry

        lax.fori_loop(1, nz, pass_z, 0)

    def last(g):
        if nz > 1:
            drain(zrecv.at[pl.ds(0, (nz - 1) * zp)], z_sem.at[g])
        acc = jnp.zeros((zp, lanes_g), F32)
        for i in range(nz):
            acc = acc + zrecv[(g * nz + i) * zp : (g * nz + i + 1) * zp, :].astype(F32)
        for i, o in enumerate(groups(ny)[g]):
            turned = pltpu.roll(acc, lanes_g - i * half, 1) if i else acc
            slot = (sum(len(h) for h in groups(ny)[:g]) + i) * zp
            ysend[slot : slot + zp, :] = turned[:, : ysend.shape[1]].astype(BF16)
            here = yrecv.at[pl.ds(mo((y * NC + c) * zp, 16), zp)]
            mine_y = ysend.at[pl.ds(slot, zp)]
            to = shard_at(o)
            if o == 0:
                yrecv[pl.ds(mo((y * NC + c) * zp, 16), zp), :] = ysend[slot : slot + zp, :]
            else:
                remote(mine_y, here, y_sem.at[0], y_sem.at[1], (to, s)).start()
            remote(mine_y, here, y_sem.at[0], y_sem.at[1], (to, sib)).start()

    back(0)
    serve_if(4, 2)
    for g, steps in enumerate(steps_of(ny)):
        for step in steps:
            if step > 2:
                gather(step)
        if g > 0:
            back(g)
    for g in range(len(groups(ny)) - 1):
        middle(g)

    drain(ptr, pt_sem.at[1])
    drain(wf.at[pl.ds(0, (ny - 1) * half)], sib_recv)
    o0 = 1 - c

    def place_pt(yk, carry):
        pt[pl.ds(mo(yk * shard + o0 * half, 16), half), :] = ptr[pl.ds(mo(yk * half, 16), half), :]
        return carry

    lax.fori_loop(0, ny, place_pt, 0)
    pooled_rows = jnp.transpose(pt[...])
    block_w = 512 if feats % 512 == 0 else feats
    keep = used[:, 0:1] > 0.0

    def project(i, carry):
        lanes = pl.ds(mo(i * block_w, 128), block_w)
        out = jnp.dot(pooled_rows, wf[:, lanes], preferred_element_type=F32) + pbias_ref[:, lanes]
        merged_ref[:, lanes] = jnp.where(keep, out, 0.0).astype(BF16)
        return carry

    lax.fori_loop(0, feats // block_w, project, 0)

    for g in range(len(groups(ny)) - 1):
        last(g)
    middle(len(groups(ny)) - 1)
    last(len(groups(ny)) - 1)
    drain(yrecv.at[pl.ds(0, (ny * NC - 1) * zp)], y_sem.at[1])
    sums = []
    for h in range(NC):
        acc = jnp.zeros((zp, yrecv.shape[1]), F32)
        for i in range(ny):
            at = (i * NC + h) * zp
            acc = acc + yrecv[at : at + zp, :].astype(F32)
        pad = jnp.zeros((zp, lanes_g - acc.shape[1]), F32)
        acc = jnp.concatenate([acc, pad], axis=1) if pad.shape[1] else acc
        lane = lax.broadcasted_iota(I32, acc.shape, 1)
        sums.append(jnp.where(lane < half, acc, 0.0))
    both = sums[0] + pltpu.roll(sums[1], half, 1)
    line = lax.broadcasted_iota(I32, both.shape, 0)
    for m in range(mper):
        for k in range(taps):
            hit = line == k * mc + c * mper + m
            one = jnp.sum(jnp.where(hit, both, 0.0), axis=0, keepdims=True)
            gw_ref[k, m : m + 1, :] = one[:, :shard]

    for way in (0, 1):
        for step in range(1, far + 1):
            for kind in (0, 1, 2):
                ring(step, way, kind).wait_send()
    drain(wf.at[pl.ds(0, (ny - 1) * half)], sib_send)
    if nx > 1:
        drain(wf.at[pl.ds(0, (ny - 1) * half), pl.ds(0, (nx - 1) * part)], share_send)
    drain(posv.at[pl.ds(0, ns - 1)], pos_sem.at[0])
    drain(arr.at[pl.ds(0, (ns - 1) * mr)], msg_sem.at[0])
    send_cot.wait_send()
    send_fr.wait_send()
    drain(pts, pt_sem.at[0])
    for g in range(len(groups(ny))):
        if nx > 1:
            drain(xrecv.at[pl.ds(0, (nx - 1) * xr)], x_send.at[g])
        if nz > 1:
            drain(zrecv.at[pl.ds(0, (nz - 1) * zp)], z_send.at[g])
    drain(yrecv.at[pl.ds(0, (ny * NC - 1) * zp)], y_sem.at[0])


def body(nx, mel_frames, positions, conv_weight, conv_bias, proj_weight, proj_bias, cotangent):
    ny, ns = lax.axis_size("dp"), lax.axis_size("seq")
    _, frames, mels = mel_frames.shape
    _, rows, feats = cotangent.shape
    taps, ch = conv_weight.shape[1:]
    tok = frames // 2
    nq = nx * NC
    nz = ns // nq
    km = taps * mels
    half = ch // ny // NC
    far = ny // 2
    n_groups = len(groups(ny))
    lanes_g = -(-max(max(len(g) for g in groups(ny)) * half, ch // ny) // 128) * 128
    lanes_y = -(-half // 128) * 128
    xr = km // nx
    zp = -(-taps * NC * (mels // ns) // 16) * 16
    cw = jnp.transpose(conv_weight, (1, 0, 2)).reshape(km, ch)
    vmem = pl.BlockSpec(memory_space=pltpu.VMEM)
    hbm = pl.BlockSpec(memory_space=pltpu.HBM)
    total = 4 * rows
    dma = pltpu.SemaphoreType.DMA
    merged, gw = pl.pallas_call(
        functools.partial(kernel, ny, ns, nx),
        out_shape=(
            jax.ShapeDtypeStruct((rows, feats), BF16),
            jax.ShapeDtypeStruct((taps, mels // ns, ch // ny), F32),
        ),
        in_specs=[hbm] * 7,
        out_specs=(vmem, vmem),
        scratch_shapes=[
            pltpu.VMEM((frames, mels), BF16),
            pltpu.VMEM((1, tok), I32),
            pltpu.VMEM((km, ch), BF16),
            pltpu.VMEM((ch,), F32),
            pltpu.VMEM((1, feats), F32),
            pltpu.VMEM((ch, feats), BF16),
            pltpu.VMEM((2 * rows, feats), BF16),
            pltpu.VMEM((ch, km), BF16),
            pltpu.VMEM((ch, 128), F32),
            pltpu.VMEM((total, mels), BF16),
            pltpu.VMEM((total, mels), BF16),
            pltpu.VMEM((ns, 1, tok), I32),
            pltpu.VMEM((4 * mels, 2 * rows), BF16),
            pltpu.VMEM((km, 4 * rows), BF16),
            pltpu.VMEM((ch, rows), BF16),
            pltpu.VMEM((ch // NC, rows), BF16),
            pltpu.VMEM((ch // NC, rows), BF16),
            pltpu.VMEM((ch // NC, 4 * rows), F32),
            pltpu.VMEM((lanes_g, 4 * rows), BF16),
            pltpu.VMEM((n_groups * km, lanes_g), BF16),
            pltpu.VMEM((n_groups * km, lanes_g), BF16),
            pltpu.VMEM((n_groups * nz * zp, lanes_g), BF16),
            pltpu.VMEM((n_groups * nz * zp, lanes_g), BF16),
            pltpu.VMEM((ny * zp, lanes_y), BF16),
            pltpu.VMEM((ny * NC * zp, lanes_y), BF16),
            dma((6 * far,)),
            dma((6 * far,)),
            dma,
            dma,
            dma,
            dma((2 * far,)),
            dma((2,)),
            dma((2,)),
            dma((2,)),
            dma((2,)),
            dma((2,)),
            dma((n_groups,)),
            dma((n_groups,)),
            dma((n_groups,)),
            dma((n_groups,)),
            dma((2,)),
            dma((7,)),
        ],
        compiler_params=pltpu.CompilerParams(
            collective_id=0, has_side_effects=True, vmem_limit_bytes=60 << 20
        ),
    )(
        mel_frames[0],
        positions,
        cw,
        conv_bias,
        proj_weight,
        proj_bias[None],
        cotangent[0],
    )
    return (merged[None], jnp.transpose(gw, (1, 0, 2)))


def solution(mesh, nx=NX):
    in_specs = (
        P("dp", "seq", None),
        P("dp", "seq"),
        P(),
        P(),
        P("dp", None),
        P(),
        P("dp", "seq", None),
    )
    out_specs = (P("dp", "seq", None), P("seq", None, "dp"))
    return jax.shard_map(
        functools.partial(body, nx), mesh=mesh, in_specs=in_specs, out_specs=out_specs, check_vma=False
    )
```

```python
import functools

import jax
import jax.numpy as jnp
from jax import lax
from jax.experimental import pallas as pl
from jax.experimental.pallas import tpu as pltpu
from jax.sharding import PartitionSpec as P

SQRT_HALF = 0.7071067811865476
INV_SQRT_TWO_PI = 0.3989422804014327
F32, BF16, I32 = jnp.float32, jnp.bfloat16, jnp.int32
MESH = pl.DeviceIdType.MESH
NT = (((1,), (1,)), ((), ()))
NX, NC = 4, 2


def mo(value, k):
    return pl.multiple_of(value, k)


def steps_of(ny):
    return {8: [[0, 1], [2], [3, 4]], 4: [[0, 1], [2]], 2: [[0], [1]]}[ny]


def groups(ny):
    far = ny // 2
    return [
        [o for t in steps for o in ([t] if t in (0, far) else [t, -t])] for steps in steps_of(ny)
    ]


def kernel(
    ny,
    ns,
    nx,
    mel_in,
    pos_in,
    cw_in,
    bias_in,
    w_ref,
    pbias_in,
    cot_ref,
    merged_ref,
    gw_ref,
    mel_ref,
    pos_ref,
    cw_ref,
    bias_ref,
    pbias_ref,
    wf,
    cot2,
    kt,
    biast,
    msgs,
    arr,
    posv,
    fr,
    xt,
    pt,
    pts,
    ptr,
    slope,
    gt,
    xsend,
    xrecv,
    zsend,
    zrecv,
    ysend,
    yrecv,
    ring_send,
    ring_recv,
    sib_send,
    sib_recv,
    share_send,
    share_recv,
    pos_sem,
    msg_sem,
    cot_sem,
    fr_sem,
    pt_sem,
    x_send,
    x_sem,
    z_send,
    z_sem,
    y_sem,
    loc_sem,
):
    nq = nx * NC
    nz = ns // nq
    frames, mels = mel_ref.shape
    tok = frames // 2
    rows = cot_ref.shape[0]
    feats = wf.shape[1]
    ch = wf.shape[0]
    shard = ch // ny
    half = shard // NC
    lanes_g = gt.shape[0]
    cap = rows // ns
    mr = 4 * cap
    km = kt.shape[1]
    taps = km // mels
    mper = mels // ns
    mc = NC * mper
    xr = km // nx
    mx = mels // nx
    zr = taps * mc
    zp = zrecv.shape[0] // (len(groups(ny)) * nz)

    y = lax.axis_index("dp")
    s = lax.axis_index("seq")
    c = lax.rem(s, NC)
    q = lax.rem(s, nq)
    z = s // nq
    x = q // NC
    sib = s + 1 - 2 * c
    up, down = lax.rem(y + 1, ny), lax.rem(y + ny - 1, ny)

    def remote(src, dst, ssem, rsem, dev):
        return pltpu.make_async_remote_copy(
            src_ref=src, dst_ref=dst, send_sem=ssem, recv_sem=rsem, device_id=dev, device_id_type=MESH
        )

    def drain(ref, sem):
        pltpu.make_async_copy(ref, ref, sem).wait()

    barrier = pltpu.get_barrier_semaphore()

    def hail_seq(i, carry):
        pl.semaphore_signal(barrier, inc=1, device_id=(y, lax.rem(s + i, ns)), device_id_type=MESH)
        return carry

    def hail_dp(i, carry):
        yt = lax.rem(y + i, ny)
        pl.semaphore_signal(barrier, inc=1, device_id=(yt, s), device_id_type=MESH)
        pl.semaphore_signal(barrier, inc=1, device_id=(yt, sib), device_id_type=MESH)
        return carry

    lax.fori_loop(1, ny, hail_dp, 0)
    lax.fori_loop(1, ns, hail_seq, 0)

    own_w = pltpu.make_async_copy(w_ref, wf.at[pl.ds(mo(y * shard, 16), shard)], loc_sem.at[0])
    own_cot = pltpu.make_async_copy(cot_ref, cot2.at[pl.ds(0, rows)], loc_sem.at[1])
    loads = [
        pltpu.make_async_copy(src, dst, loc_sem.at[2 + i])
        for i, (src, dst) in enumerate(
            [
                (pos_in, pos_ref),
                (mel_in, mel_ref),
                (cw_in, cw_ref),
                (bias_in, bias_ref),
                (pbias_in, pbias_ref),
            ]
        )
    ]
    for load in loads:
        load.start()
    own_w.start()
    own_cot.start()
    loads[0].wait()
    loads[1].wait()

    before = (
        lax.broadcasted_iota(I32, (tok, tok), 0) < lax.broadcasted_iota(I32, (tok, tok), 1)
    ).astype(BF16)
    total = ns * mr

    def spread(hit, value):
        hit_b = hit.astype(F32).astype(BF16)
        rank = jnp.dot(hit_b, before, preferred_element_type=F32)
        lane = lax.broadcasted_iota(I32, (ns, 128), 1)
        table = jnp.zeros((ns, 128), F32)
        for k in range(cap):
            entry = jnp.sum(jnp.where(hit & (rank == k), value + 1.0, 0.0), axis=1, keepdims=True)
            table = table + jnp.where(lane == k, entry, 0.0)
        group = lax.broadcasted_iota(I32, (total, ns), 0) // mr
        expand = (group == lax.broadcasted_iota(I32, (total, ns), 1)).astype(F32).astype(BF16)
        wide = jnp.dot(expand, table.astype(BF16), preferred_element_type=F32)
        n = lax.broadcasted_iota(I32, (total, 128), 0)
        chosen = lax.broadcasted_iota(I32, (total, 128), 1) == lax.rem(n // 4, cap)
        return jnp.sum(jnp.where(chosen, wide, 0.0), axis=1, keepdims=True)

    pos_row = jnp.broadcast_to(pos_ref[...], (ns, tok))
    to_dest = (pos_row // rows) == lax.broadcasted_iota(I32, (ns, tok), 0)
    token = spread(to_dest, lax.broadcasted_iota(I32, (ns, tok), 1).astype(F32))
    n_col = lax.broadcasted_iota(I32, (total, 1), 0)
    f_col = lax.rem(n_col, 4).astype(F32)
    frame = jnp.where(token > 0.0, 2.0 * (token - 1.0) - 1.0 + f_col, -100.0)
    pick = (lax.broadcasted_iota(I32, (total, frames), 1).astype(F32) == frame).astype(F32)
    p = lax.broadcasted_iota(I32, (mels, mels), 1)
    from_m = lax.rem(p // mc, nz) * (nx * mc) + (p // mx) * mc + lax.rem(p, mc)
    order = (lax.broadcasted_iota(I32, (mels, mels), 0) == from_m).astype(F32).astype(BF16)
    mel_p = jnp.dot(mel_ref[...], order, preferred_element_type=F32).astype(BF16)
    msgs[...] = jnp.dot(pick.astype(BF16), mel_p, preferred_element_type=F32).astype(BF16)
    own_slot = pl.ds(mo(s * mr, 16), mr)
    arr[own_slot, :] = msgs[own_slot, :]
    posv[s] = pos_ref[...]

    for load in loads[2:]:
        load.wait()
    for k in range(taps):
        turned = jnp.transpose(cw_ref[k * mels : (k + 1) * mels, :])
        kt[:, k * mels : (k + 1) * mels] = jnp.dot(
            turned, order, preferred_element_type=F32
        ).astype(BF16)
    for i in range(ch // 128):
        block = jnp.broadcast_to(bias_ref[128 * i : 128 * (i + 1)][None, :], (128, 128))
        biast[128 * i : 128 * (i + 1), :] = jnp.transpose(block)
    gt[...] = jnp.zeros_like(gt)

    own_w.wait()
    pl.semaphore_wait(barrier, 2 * (ny - 1) + ns - 1)

    far = ny // 2
    cut = -(-(half // 2) // 16) * 16

    shared = feats // 2
    part = shared // nx

    def wrows(owner, lo, size):
        return wf.at[pl.ds(mo(owner * shard + c * half + lo, 16), size)]

    def span(step, way):
        if step < far:
            return 0, half
        return (0, cut) if way == 0 else (cut, half - cut)

    def piece(owner, step, way, kind):
        lo, size = span(step, way)
        row = pl.ds(mo(owner * shard + c * half + lo, 16), size)
        if kind == 0:
            return wf.at[row, pl.ds(mo(shared + x * part, 128), part)]
        return wf.at[row, pl.ds((kind - 1) * (shared // 2), shared // 2)]

    def ring_sem(step, way, kind):
        return (way * far + step - 1) * 3 + kind

    def ring(step, way, kind):
        owner = lax.rem(y + ny + 1 - step if way == 0 else y + step - 1, ny)
        ref = piece(owner, step, way, kind)
        i = ring_sem(step, way, kind)
        target = (up, s) if way == 0 else (down, s)
        return remote(ref, ref, ring_send.at[i], ring_recv.at[i], target)

    def source(step, way):
        return lax.rem(y + ny - step if way == 0 else y + step, ny)

    def serve(step, kind):
        for way in (0, 1):
            ref = piece(source(step, way), step, way, kind)
            pltpu.make_async_copy(ref, ref, ring_recv.at[ring_sem(step, way, kind)]).wait()
            if step < far:
                ring(step + 1, way, kind).start()
            if kind:
                remote(ref, ref, sib_send, sib_recv, (y, sib)).start()
            else:
                for t in range(1, nx):
                    to = lax.rem(x + t, nx)
                    remote(
                        ref,
                        ref,
                        share_send,
                        share_recv.at[way * far + step - 1],
                        (y, z * nq + to * NC + c),
                    ).start()

    def gather(step):
        for way in (0, 1):
            lo, size = span(step, way)
            row = pl.ds(mo(source(step, way) * shard + c * half + lo, 16), size)
            if nx > 1:
                drain(wf.at[row, pl.ds(0, (nx - 1) * part)], share_recv.at[way * far + step - 1])
            ref = wf.at[row, pl.ds(shared, shared)]
            remote(ref, ref, sib_send, sib_recv, (y, sib)).start()

    for kind in (0, 1, 2):
        for way in (0, 1):
            ring(1, way, kind).start()

    def post(i, carry):
        hop = (i + 1) // 2
        to = lax.rem(s + ns + hop * (2 * lax.rem(i, 2) - 1), ns)
        remote(posv.at[s], posv.at[s], pos_sem.at[0], pos_sem.at[1], (y, to)).start()
        remote(
            msgs.at[pl.ds(mo(to * mr, 16), mr)],
            arr.at[pl.ds(mo(s * mr, 16), mr)],
            msg_sem.at[0],
            msg_sem.at[1],
            (y, to),
        ).start()
        return carry

    lax.fori_loop(1, ns, post, 0)
    send_cot = remote(
        cot_ref, cot2.at[pl.ds(rows, rows)], cot_sem.at[0], cot_sem.at[1], (y, sib)
    )
    send_cot.start()

    def serve_if(step, kind):
        if step <= far:
            serve(step, kind)

    serve(1, 0)
    serve(1, 1)
    serve(1, 2)
    serve_if(2, 0)
    serve_if(2, 1)
    drain(posv.at[pl.ds(0, ns - 1)], pos_sem.at[1])
    all_pos = jnp.reshape(posv[...], (ns, tok))
    mine = (all_pos // rows) == s
    slot_row = spread(mine, lax.rem(all_pos, rows).astype(F32)) - 1.0
    row_lane = lax.broadcasted_iota(I32, (total, rows), 1).astype(F32)
    at_row = row_lane == slot_row
    n_f = lax.rem(lax.broadcasted_iota(I32, (total, rows), 0), 4)
    places = [(at_row & (n_f == f)).astype(F32).astype(BF16) for f in range(4)]
    used = lax.dot_general(
        places[0], jnp.ones((total, 128), BF16), (((0,), (0,)), ((), ())), preferred_element_type=F32
    )
    drain(arr.at[pl.ds(0, (ns - 1) * mr)], msg_sem.at[1])
    arr_t = jnp.transpose(arr[...])
    for f in range(4):
        fr[f * mels : (f + 1) * mels, 0:rows] = jnp.dot(arr_t, places[f], preferred_element_type=F32).astype(BF16)
    send_fr = remote(
        fr.at[:, pl.ds(0, rows)], fr.at[:, pl.ds(rows, rows)], fr_sem.at[0], fr_sem.at[1], (y, sib)
    )
    send_fr.start()
    serve_if(2, 2)
    serve_if(3, 0)
    send_fr.wait_recv()
    wide = 2 * rows
    for j in range(2):
        for xx in range(nx):
            for k in range(taps):
                at = xx * xr + k * mx
                xt[at : at + mx, j * wide : (j + 1) * wide] = fr[
                    (j + k) * mels + xx * mx : (j + k) * mels + (xx + 1) * mx, :
                ]

    def stem(yk, carry):
        r0 = mo(yk * shard + c * half, 16)
        l0 = mo(yk * half, 16)
        weights = kt[pl.ds(r0, half), :]
        b = biast[pl.ds(r0, half), :]
        for block in range(wide // 128):
            at = block * 128
            values, slopes = [], []
            for j in range(2):
                lanes = pl.ds(j * wide + at, 128)
                window = fr[j * mels : j * mels + km, at : at + 128]
                v = jnp.dot(weights, window, preferred_element_type=F32) + b
                phi = 0.5 + 0.5 * lax.erf(v * SQRT_HALF)
                values.append(v * phi)
                slope[pl.ds(l0, half), lanes] = 0.5 * phi + v * (0.5 * INV_SQRT_TWO_PI) * jnp.exp(
                    -0.5 * v * v
                )
            pooled = (0.5 * (values[0] + values[1])).astype(BF16)
            if at < rows:
                pt[pl.ds(r0, half), at : at + 128] = pooled
            else:
                pts[pl.ds(l0, half), at - rows : at - rows + 128] = pooled
        remote(
            pts.at[pl.ds(l0, half)], ptr.at[pl.ds(l0, half)], pt_sem.at[0], pt_sem.at[1], (y, sib)
        ).start()
        return carry

    serve_if(3, 1)
    gather(1)
    serve_if(4, 0)
    lax.fori_loop(0, ny // 4, stem, 0)
    serve_if(3, 2)
    if far > 1:
        gather(2)
    lax.fori_loop(ny // 4, ny - ny // 4, stem, 0)
    serve_if(4, 1)
    lax.fori_loop(ny - ny // 4, ny, stem, 0)
    own_cot.wait()
    send_cot.wait_recv()

    def shard_at(offset):
        return lax.rem(y + ny + offset, ny)

    def back(g):
        offsets = groups(ny)[g]
        w = jnp.concatenate([wrows(shard_at(o), 0, half)[...] for o in offsets], axis=0)
        gp = lax.dot_general(w, cot2[...], NT, preferred_element_type=F32).astype(BF16).astype(F32)
        for i, o in enumerate(offsets):
            l0 = mo(shard_at(o) * half, 16)
            for j in range(2):
                lanes = slice(j * wide, (j + 1) * wide)
                grad = gp[i * half : (i + 1) * half] * slope[pl.ds(l0, half), lanes]
                gt[i * half : (i + 1) * half, lanes] = grad.astype(BF16)
        product = lax.dot_general(xt[...], gt[...], NT, preferred_element_type=F32)
        xsend[g * km : (g + 1) * km, :] = product.astype(BF16)
        mine_x = pl.ds(mo((g * nx + x) * xr, 16), xr)
        xrecv[mine_x, :] = xsend[pl.ds(mo(g * km + x * xr, 16), xr), :]

        def pass_x(t, carry):
            to = lax.rem(x + t, nx)
            remote(
                xsend.at[pl.ds(mo(g * km + to * xr, 16), xr)],
                xrecv.at[mine_x],
                x_send.at[g],
                x_sem.at[g],
                (y, z * nq + to * NC + c),
            ).start()
            return carry

        lax.fori_loop(1, nx, pass_x, 0)

    n_new = lax.broadcasted_iota(I32, (nz * zp, xr), 0)
    in_z = lax.rem(n_new, zp)
    old = (in_z // mc) * mx + (n_new // zp) * mc + lax.rem(in_z, mc)
    regroup = (
        ((lax.broadcasted_iota(I32, (nz * zp, xr), 1) == old) & (in_z < zr)).astype(F32).astype(BF16)
    )

    def middle(g):
        if nx > 1:
            drain(xrecv.at[pl.ds(0, (nx - 1) * xr)], x_sem.at[g])
        acc = jnp.zeros((xr, lanes_g), F32)
        for i in range(nx):
            acc = acc + xrecv[(g * nx + i) * xr : (g * nx + i + 1) * xr, :].astype(F32)
        zsend[g * nz * zp : (g + 1) * nz * zp, :] = jnp.dot(
            regroup, acc.astype(BF16), preferred_element_type=F32
        ).astype(BF16)
        mine_z = pl.ds(mo((g * nz + z) * zp, 16), zp)
        zrecv[mine_z, :] = zsend[mine_z, :]

        def pass_z(t, carry):
            hop = (t + 1) // 2
            to = lax.rem(z + nz + hop * (2 * lax.rem(t, 2) - 1), nz)
            remote(
                zsend.at[pl.ds(mo((g * nz + to) * zp, 16), zp)],
                zrecv.at[mine_z],
                z_send.at[g],
                z_sem.at[g],
                (y, to * nq + q),
            ).start()
            return carry

        lax.fori_loop(1, nz, pass_z, 0)

    def last(g):
        if nz > 1:
            drain(zrecv.at[pl.ds(0, (nz - 1) * zp)], z_sem.at[g])
        acc = jnp.zeros((zp, lanes_g), F32)
        for i in range(nz):
            acc = acc + zrecv[(g * nz + i) * zp : (g * nz + i + 1) * zp, :].astype(F32)
        for i, o in enumerate(groups(ny)[g]):
            turned = pltpu.roll(acc, lanes_g - i * half, 1) if i else acc
            slot = (sum(len(h) for h in groups(ny)[:g]) + i) * zp
            ysend[slot : slot + zp, :] = turned[:, : ysend.shape[1]].astype(BF16)
            here = yrecv.at[pl.ds(mo((y * NC + c) * zp, 16), zp)]
            mine_y = ysend.at[pl.ds(slot, zp)]
            to = shard_at(o)
            if o == 0:
                yrecv[pl.ds(mo((y * NC + c) * zp, 16), zp), :] = ysend[slot : slot + zp, :]
            else:
                remote(mine_y, here, y_sem.at[0], y_sem.at[1], (to, s)).start()
            remote(mine_y, here, y_sem.at[0], y_sem.at[1], (to, sib)).start()

    back(0)
    serve_if(4, 2)
    for g, steps in enumerate(steps_of(ny)):
        for step in steps:
            if step > 2:
                gather(step)
        if g > 0:
            back(g)
    for g in range(len(groups(ny)) - 1):
        middle(g)

    drain(ptr, pt_sem.at[1])
    drain(wf.at[pl.ds(0, (ny - 1) * half)], sib_recv)
    o0 = 1 - c

    def place_pt(yk, carry):
        pt[pl.ds(mo(yk * shard + o0 * half, 16), half), :] = ptr[pl.ds(mo(yk * half, 16), half), :]
        return carry

    lax.fori_loop(0, ny, place_pt, 0)
    pooled_rows = jnp.transpose(pt[...])
    block_w = 512 if feats % 512 == 0 else feats
    keep = used[:, 0:1] > 0.0

    def project(i, carry):
        lanes = pl.ds(mo(i * block_w, 128), block_w)
        out = jnp.dot(pooled_rows, wf[:, lanes], preferred_element_type=F32) + pbias_ref[:, lanes]
        merged_ref[:, lanes] = jnp.where(keep, out, 0.0).astype(BF16)
        return carry

    blocks = feats // block_w
    lax.fori_loop(0, blocks // 2, project, 0)

    middle(len(groups(ny)) - 1)
    for g in range(len(groups(ny)) - 1):
        last(g)
    lax.fori_loop(blocks // 2, blocks, project, 0)
    last(len(groups(ny)) - 1)
    drain(yrecv.at[pl.ds(0, (ny * NC - 1) * zp)], y_sem.at[1])
    sums = []
    for h in range(NC):
        acc = jnp.zeros((zp, yrecv.shape[1]), F32)
        for i in range(ny):
            at = (i * NC + h) * zp
            acc = acc + yrecv[at : at + zp, :].astype(F32)
        pad = jnp.zeros((zp, lanes_g - acc.shape[1]), F32)
        acc = jnp.concatenate([acc, pad], axis=1) if pad.shape[1] else acc
        lane = lax.broadcasted_iota(I32, acc.shape, 1)
        sums.append(jnp.where(lane < half, acc, 0.0))
    both = sums[0] + pltpu.roll(sums[1], half, 1)
    line = lax.broadcasted_iota(I32, both.shape, 0)
    for m in range(mper):
        for k in range(taps):
            hit = line == k * mc + c * mper + m
            one = jnp.sum(jnp.where(hit, both, 0.0), axis=0, keepdims=True)
            gw_ref[k, m : m + 1, :] = one[:, :shard]

    for way in (0, 1):
        for step in range(1, far + 1):
            for kind in (0, 1, 2):
                ring(step, way, kind).wait_send()
    drain(wf.at[pl.ds(0, (ny - 1) * half)], sib_send)
    if nx > 1:
        drain(wf.at[pl.ds(0, (ny - 1) * half), pl.ds(0, (nx - 1) * part)], share_send)
    drain(posv.at[pl.ds(0, ns - 1)], pos_sem.at[0])
    drain(arr.at[pl.ds(0, (ns - 1) * mr)], msg_sem.at[0])
    send_cot.wait_send()
    send_fr.wait_send()
    drain(pts, pt_sem.at[0])
    for g in range(len(groups(ny))):
        if nx > 1:
            drain(xrecv.at[pl.ds(0, (nx - 1) * xr)], x_send.at[g])
        if nz > 1:
            drain(zrecv.at[pl.ds(0, (nz - 1) * zp)], z_send.at[g])
    drain(yrecv.at[pl.ds(0, (ny * NC - 1) * zp)], y_sem.at[0])


def body(nx, mel_frames, positions, conv_weight, conv_bias, proj_weight, proj_bias, cotangent):
    ny, ns = lax.axis_size("dp"), lax.axis_size("seq")
    _, frames, mels = mel_frames.shape
    _, rows, feats = cotangent.shape
    taps, ch = conv_weight.shape[1:]
    tok = frames // 2
    nq = nx * NC
    nz = ns // nq
    km = taps * mels
    half = ch // ny // NC
    far = ny // 2
    n_groups = len(groups(ny))
    lanes_g = -(-max(max(len(g) for g in groups(ny)) * half, ch // ny) // 128) * 128
    lanes_y = -(-half // 128) * 128
    xr = km // nx
    zp = -(-taps * NC * (mels // ns) // 16) * 16
    cw = jnp.transpose(conv_weight, (1, 0, 2)).reshape(km, ch)
    vmem = pl.BlockSpec(memory_space=pltpu.VMEM)
    hbm = pl.BlockSpec(memory_space=pltpu.HBM)
    total = 4 * rows
    dma = pltpu.SemaphoreType.DMA
    merged, gw = pl.pallas_call(
        functools.partial(kernel, ny, ns, nx),
        out_shape=(
            jax.ShapeDtypeStruct((rows, feats), BF16),
            jax.ShapeDtypeStruct((taps, mels // ns, ch // ny), F32),
        ),
        in_specs=[hbm] * 7,
        out_specs=(vmem, vmem),
        scratch_shapes=[
            pltpu.VMEM((frames, mels), BF16),
            pltpu.VMEM((1, tok), I32),
            pltpu.VMEM((km, ch), BF16),
            pltpu.VMEM((ch,), F32),
            pltpu.VMEM((1, feats), F32),
            pltpu.VMEM((ch, feats), BF16),
            pltpu.VMEM((2 * rows, feats), BF16),
            pltpu.VMEM((ch, km), BF16),
            pltpu.VMEM((ch, 128), F32),
            pltpu.VMEM((total, mels), BF16),
            pltpu.VMEM((total, mels), BF16),
            pltpu.VMEM((ns, 1, tok), I32),
            pltpu.VMEM((4 * mels, 2 * rows), BF16),
            pltpu.VMEM((km, 4 * rows), BF16),
            pltpu.VMEM((ch, rows), BF16),
            pltpu.VMEM((ch // NC, rows), BF16),
            pltpu.VMEM((ch // NC, rows), BF16),
            pltpu.VMEM((ch // NC, 4 * rows), F32),
            pltpu.VMEM((lanes_g, 4 * rows), BF16),
            pltpu.VMEM((n_groups * km, lanes_g), BF16),
            pltpu.VMEM((n_groups * km, lanes_g), BF16),
            pltpu.VMEM((n_groups * nz * zp, lanes_g), BF16),
            pltpu.VMEM((n_groups * nz * zp, lanes_g), BF16),
            pltpu.VMEM((ny * zp, lanes_y), BF16),
            pltpu.VMEM((ny * NC * zp, lanes_y), BF16),
            dma((6 * far,)),
            dma((6 * far,)),
            dma,
            dma,
            dma,
            dma((2 * far,)),
            dma((2,)),
            dma((2,)),
            dma((2,)),
            dma((2,)),
            dma((2,)),
            dma((n_groups,)),
            dma((n_groups,)),
            dma((n_groups,)),
            dma((n_groups,)),
            dma((2,)),
            dma((7,)),
        ],
        compiler_params=pltpu.CompilerParams(
            collective_id=0, has_side_effects=True, vmem_limit_bytes=44 << 20
        ),
    )(
        mel_frames[0],
        positions,
        cw,
        conv_bias,
        proj_weight,
        proj_bias[None],
        cotangent[0],
    )
    return (merged[None], jnp.transpose(gw, (1, 0, 2)))


def solution(mesh, nx=NX):
    in_specs = (
        P("dp", "seq", None),
        P("dp", "seq"),
        P(),
        P(),
        P("dp", None),
        P(),
        P("dp", "seq", None),
    )
    out_specs = (P("dp", "seq", None), P("seq", None, "dp"))
    return jax.shard_map(
        functools.partial(body, nx), mesh=mesh, in_specs=in_specs, out_specs=out_specs, check_vma=False
    )
```

```python
import functools

import jax
import jax.numpy as jnp
from jax import lax
from jax.experimental import pallas as pl
from jax.experimental.pallas import tpu as pltpu
from jax.sharding import PartitionSpec as P

SQRT_HALF = 0.7071067811865476
INV_SQRT_TWO_PI = 0.3989422804014327
F32, BF16, I32 = jnp.float32, jnp.bfloat16, jnp.int32
MESH = pl.DeviceIdType.MESH
NT = (((1,), (1,)), ((), ()))
NX, NC = 4, 2


def mo(value, k):
    return pl.multiple_of(value, k)


def steps_of(ny):
    return {8: [[0, 1], [2], [3, 4]], 4: [[0, 1], [2]], 2: [[0], [1]]}[ny]


def groups(ny):
    far = ny // 2
    return [
        [o for t in steps for o in ([t] if t in (0, far) else [t, -t])] for steps in steps_of(ny)
    ]


def kernel(
    ny,
    ns,
    nx,
    mel_in,
    pos_in,
    cw_in,
    bias_in,
    w_ref,
    pbias_in,
    cot_ref,
    merged_ref,
    gw_ref,
    mel_ref,
    pos_ref,
    cw_ref,
    bias_ref,
    pbias_ref,
    wf,
    cot2,
    kt,
    biast,
    msgs,
    arr,
    posv,
    fr,
    xt,
    pt,
    pts,
    ptr,
    slope,
    gt,
    xsend,
    xrecv,
    zsend,
    zrecv,
    ysend,
    yrecv,
    ring_send,
    ring_recv,
    sib_send,
    sib_recv,
    share_send,
    share_recv,
    pos_sem,
    msg_sem,
    cot_sem,
    fr_sem,
    pt_sem,
    x_send,
    x_sem,
    z_send,
    z_sem,
    y_sem,
    loc_sem,
):
    nq = nx * NC
    nz = ns // nq
    frames, mels = mel_ref.shape
    tok = frames // 2
    rows = cot_ref.shape[0]
    feats = wf.shape[1]
    ch = wf.shape[0]
    shard = ch // ny
    half = shard // NC
    lanes_g = gt.shape[0]
    cap = rows // ns
    mr = 4 * cap
    km = kt.shape[1]
    taps = km // mels
    mper = mels // ns
    mc = NC * mper
    xr = km // nx
    mx = mels // nx
    zr = taps * mc
    zp = zrecv.shape[0] // (len(groups(ny)) * nz)

    y = lax.axis_index("dp")
    s = lax.axis_index("seq")
    c = lax.rem(s, NC)
    q = lax.rem(s, nq)
    z = s // nq
    x = q // NC
    sib = s + 1 - 2 * c
    up, down = lax.rem(y + 1, ny), lax.rem(y + ny - 1, ny)

    def remote(src, dst, ssem, rsem, dev):
        return pltpu.make_async_remote_copy(
            src_ref=src, dst_ref=dst, send_sem=ssem, recv_sem=rsem, device_id=dev, device_id_type=MESH
        )

    def drain(ref, sem):
        pltpu.make_async_copy(ref, ref, sem).wait()

    barrier = pltpu.get_barrier_semaphore()

    def hail_seq(i, carry):
        pl.semaphore_signal(barrier, inc=1, device_id=(y, lax.rem(s + i, ns)), device_id_type=MESH)
        return carry

    def hail_dp(i, carry):
        yt = lax.rem(y + i, ny)
        pl.semaphore_signal(barrier, inc=1, device_id=(yt, s), device_id_type=MESH)
        pl.semaphore_signal(barrier, inc=1, device_id=(yt, sib), device_id_type=MESH)
        return carry

    lax.fori_loop(1, ny, hail_dp, 0)
    lax.fori_loop(1, ns, hail_seq, 0)

    own_w = pltpu.make_async_copy(w_ref, wf.at[pl.ds(mo(y * shard, 16), shard)], loc_sem.at[0])
    own_cot = pltpu.make_async_copy(cot_ref, cot2.at[pl.ds(0, rows)], loc_sem.at[1])
    loads = [
        pltpu.make_async_copy(src, dst, loc_sem.at[2 + i])
        for i, (src, dst) in enumerate(
            [
                (pos_in, pos_ref),
                (mel_in, mel_ref),
                (cw_in, cw_ref),
                (bias_in, bias_ref),
                (pbias_in, pbias_ref),
            ]
        )
    ]
    for load in loads:
        load.start()
    own_w.start()
    own_cot.start()
    loads[0].wait()
    loads[1].wait()

    before = (
        lax.broadcasted_iota(I32, (tok, tok), 0) < lax.broadcasted_iota(I32, (tok, tok), 1)
    ).astype(BF16)
    total = ns * mr

    def spread(hit, value):
        hit_b = hit.astype(F32).astype(BF16)
        rank = jnp.dot(hit_b, before, preferred_element_type=F32)
        lane = lax.broadcasted_iota(I32, (ns, 128), 1)
        table = jnp.zeros((ns, 128), F32)
        for k in range(cap):
            entry = jnp.sum(jnp.where(hit & (rank == k), value + 1.0, 0.0), axis=1, keepdims=True)
            table = table + jnp.where(lane == k, entry, 0.0)
        group = lax.broadcasted_iota(I32, (total, ns), 0) // mr
        expand = (group == lax.broadcasted_iota(I32, (total, ns), 1)).astype(F32).astype(BF16)
        wide = jnp.dot(expand, table.astype(BF16), preferred_element_type=F32)
        n = lax.broadcasted_iota(I32, (total, 128), 0)
        chosen = lax.broadcasted_iota(I32, (total, 128), 1) == lax.rem(n // 4, cap)
        return jnp.sum(jnp.where(chosen, wide, 0.0), axis=1, keepdims=True)

    pos_row = jnp.broadcast_to(pos_ref[...], (ns, tok))
    to_dest = (pos_row // rows) == lax.broadcasted_iota(I32, (ns, tok), 0)
    token = spread(to_dest, lax.broadcasted_iota(I32, (ns, tok), 1).astype(F32))
    n_col = lax.broadcasted_iota(I32, (total, 1), 0)
    f_col = lax.rem(n_col, 4).astype(F32)
    frame = jnp.where(token > 0.0, 2.0 * (token - 1.0) - 1.0 + f_col, -100.0)
    pick = (lax.broadcasted_iota(I32, (total, frames), 1).astype(F32) == frame).astype(F32)
    p = lax.broadcasted_iota(I32, (mels, mels), 1)
    from_m = lax.rem(p // mc, nz) * (nx * mc) + (p // mx) * mc + lax.rem(p, mc)
    order = (lax.broadcasted_iota(I32, (mels, mels), 0) == from_m).astype(F32).astype(BF16)
    mel_p = jnp.dot(mel_ref[...], order, preferred_element_type=F32).astype(BF16)
    msgs[...] = jnp.dot(pick.astype(BF16), mel_p, preferred_element_type=F32).astype(BF16)
    own_slot = pl.ds(mo(s * mr, 16), mr)
    arr[own_slot, :] = msgs[own_slot, :]
    posv[s] = pos_ref[...]

    for load in loads[2:]:
        load.wait()
    for k in range(taps):
        turned = jnp.transpose(cw_ref[k * mels : (k + 1) * mels, :])
        kt[:, k * mels : (k + 1) * mels] = jnp.dot(
            turned, order, preferred_element_type=F32
        ).astype(BF16)
    for i in range(ch // 128):
        block = jnp.broadcast_to(bias_ref[128 * i : 128 * (i + 1)][None, :], (128, 128))
        biast[128 * i : 128 * (i + 1), :] = jnp.transpose(block)
    gt[...] = jnp.zeros_like(gt)

    own_w.wait()
    pl.semaphore_wait(barrier, 2 * (ny - 1) + ns - 1)

    far = ny // 2
    cut = -(-(half // 2) // 16) * 16

    shared = feats // 2
    part = shared // nx

    def wrows(owner, lo, size):
        return wf.at[pl.ds(mo(owner * shard + c * half + lo, 16), size)]

    def span(step, way):
        if step < far:
            return 0, half
        return (0, cut) if way == 0 else (cut, half - cut)

    def piece(owner, step, way, kind):
        lo, size = span(step, way)
        row = pl.ds(mo(owner * shard + c * half + lo, 16), size)
        if kind == 0:
            return wf.at[row, pl.ds(mo(shared + x * part, 128), part)]
        return wf.at[row, pl.ds((kind - 1) * (shared // 2), shared // 2)]

    def ring_sem(step, way, kind):
        return (way * far + step - 1) * 3 + kind

    def ring(step, way, kind):
        owner = lax.rem(y + ny + 1 - step if way == 0 else y + step - 1, ny)
        ref = piece(owner, step, way, kind)
        i = ring_sem(step, way, kind)
        target = (up, s) if way == 0 else (down, s)
        return remote(ref, ref, ring_send.at[i], ring_recv.at[i], target)

    def source(step, way):
        return lax.rem(y + ny - step if way == 0 else y + step, ny)

    def serve(step, kind):
        for way in (0, 1):
            ref = piece(source(step, way), step, way, kind)
            pltpu.make_async_copy(ref, ref, ring_recv.at[ring_sem(step, way, kind)]).wait()
            if step < far:
                ring(step + 1, way, kind).start()
            if kind:
                remote(ref, ref, sib_send, sib_recv, (y, sib)).start()
            else:
                for t in range(1, nx):
                    to = lax.rem(x + t, nx)
                    remote(
                        ref,
                        ref,
                        share_send,
                        share_recv.at[way * far + step - 1],
                        (y, z * nq + to * NC + c),
                    ).start()

    def gather(step):
        for way in (0, 1):
            lo, size = span(step, way)
            row = pl.ds(mo(source(step, way) * shard + c * half + lo, 16), size)
            if nx > 1:
                drain(wf.at[row, pl.ds(0, (nx - 1) * part)], share_recv.at[way * far + step - 1])
            ref = wf.at[row, pl.ds(shared, shared)]
            remote(ref, ref, sib_send, sib_recv, (y, sib)).start()

    for kind in (0, 1, 2):
        for way in (0, 1):
            ring(1, way, kind).start()

    def post(i, carry):
        hop = (i + 1) // 2
        to = lax.rem(s + ns + hop * (2 * lax.rem(i, 2) - 1), ns)
        remote(posv.at[s], posv.at[s], pos_sem.at[0], pos_sem.at[1], (y, to)).start()
        remote(
            msgs.at[pl.ds(mo(to * mr, 16), mr)],
            arr.at[pl.ds(mo(s * mr, 16), mr)],
            msg_sem.at[0],
            msg_sem.at[1],
            (y, to),
        ).start()
        return carry

    lax.fori_loop(1, ns, post, 0)
    send_cot = remote(
        cot_ref, cot2.at[pl.ds(rows, rows)], cot_sem.at[0], cot_sem.at[1], (y, sib)
    )
    send_cot.start()

    def serve_if(step, kind):
        if step <= far:
            serve(step, kind)

    serve(1, 0)
    serve(1, 1)
    serve(1, 2)
    serve_if(2, 0)
    serve_if(2, 1)
    drain(posv.at[pl.ds(0, ns - 1)], pos_sem.at[1])
    all_pos = jnp.reshape(posv[...], (ns, tok))
    mine = (all_pos // rows) == s
    slot_row = spread(mine, lax.rem(all_pos, rows).astype(F32)) - 1.0
    row_lane = lax.broadcasted_iota(I32, (total, rows), 1).astype(F32)
    at_row = row_lane == slot_row
    n_f = lax.rem(lax.broadcasted_iota(I32, (total, rows), 0), 4)
    places = [(at_row & (n_f == f)).astype(F32).astype(BF16) for f in range(4)]
    used = lax.dot_general(
        places[0], jnp.ones((total, 128), BF16), (((0,), (0,)), ((), ())), preferred_element_type=F32
    )
    drain(arr.at[pl.ds(0, (ns - 1) * mr)], msg_sem.at[1])
    arr_t = jnp.transpose(arr[...])
    for f in range(4):
        fr[f * mels : (f + 1) * mels, 0:rows] = jnp.dot(arr_t, places[f], preferred_element_type=F32).astype(BF16)
    send_fr = remote(
        fr.at[:, pl.ds(0, rows)], fr.at[:, pl.ds(rows, rows)], fr_sem.at[0], fr_sem.at[1], (y, sib)
    )
    send_fr.start()
    serve_if(2, 2)
    serve_if(3, 0)
    send_fr.wait_recv()
    wide = 2 * rows
    for j in range(2):
        for xx in range(nx):
            for k in range(taps):
                at = xx * xr + k * mx
                xt[at : at + mx, j * wide : (j + 1) * wide] = fr[
                    (j + k) * mels + xx * mx : (j + k) * mels + (xx + 1) * mx, :
                ]

    def stem(yk, carry):
        r0 = mo(yk * shard + c * half, 16)
        l0 = mo(yk * half, 16)
        weights = kt[pl.ds(r0, half), :]
        b = biast[pl.ds(r0, half), :]
        for block in range(wide // 128):
            at = block * 128
            values, slopes = [], []
            for j in range(2):
                lanes = pl.ds(j * wide + at, 128)
                window = fr[j * mels : j * mels + km, at : at + 128]
                v = jnp.dot(weights, window, preferred_element_type=F32) + b
                phi = 0.5 + 0.5 * lax.erf(v * SQRT_HALF)
                values.append(v * phi)
                slope[pl.ds(l0, half), lanes] = 0.5 * phi + v * (0.5 * INV_SQRT_TWO_PI) * jnp.exp(
                    -0.5 * v * v
                )
            pooled = (0.5 * (values[0] + values[1])).astype(BF16)
            if at < rows:
                pt[pl.ds(r0, half), at : at + 128] = pooled
            else:
                pts[pl.ds(l0, half), at - rows : at - rows + 128] = pooled
        remote(
            pts.at[pl.ds(l0, half)], ptr.at[pl.ds(l0, half)], pt_sem.at[0], pt_sem.at[1], (y, sib)
        ).start()
        return carry

    serve_if(3, 1)
    gather(1)
    serve_if(4, 0)
    lax.fori_loop(0, ny // 4, stem, 0)
    serve_if(3, 2)
    if far > 1:
        gather(2)
    lax.fori_loop(ny // 4, ny - ny // 4, stem, 0)
    serve_if(4, 1)
    lax.fori_loop(ny - ny // 4, ny, stem, 0)
    own_cot.wait()
    send_cot.wait_recv()

    def shard_at(offset):
        return lax.rem(y + ny + offset, ny)

    def back(g):
        offsets = groups(ny)[g]
        w = jnp.concatenate([wrows(shard_at(o), 0, half)[...] for o in offsets], axis=0)
        gp = lax.dot_general(w, cot2[...], NT, preferred_element_type=F32).astype(BF16).astype(F32)
        for i, o in enumerate(offsets):
            l0 = mo(shard_at(o) * half, 16)
            for j in range(2):
                lanes = slice(j * wide, (j + 1) * wide)
                grad = gp[i * half : (i + 1) * half] * slope[pl.ds(l0, half), lanes]
                gt[i * half : (i + 1) * half, lanes] = grad.astype(BF16)
        product = lax.dot_general(xt[...], gt[...], NT, preferred_element_type=F32)
        xsend[g * km : (g + 1) * km, :] = product.astype(BF16)
        mine_x = pl.ds(mo((g * nx + x) * xr, 16), xr)
        xrecv[mine_x, :] = xsend[pl.ds(mo(g * km + x * xr, 16), xr), :]

        def pass_x(t, carry):
            to = lax.rem(x + t, nx)
            remote(
                xsend.at[pl.ds(mo(g * km + to * xr, 16), xr)],
                xrecv.at[mine_x],
                x_send.at[g],
                x_sem.at[g],
                (y, z * nq + to * NC + c),
            ).start()
            return carry

        lax.fori_loop(1, nx, pass_x, 0)

    n_new = lax.broadcasted_iota(I32, (nz * zp, xr), 0)
    in_z = lax.rem(n_new, zp)
    old = (in_z // mc) * mx + (n_new // zp) * mc + lax.rem(in_z, mc)
    regroup = (
        ((lax.broadcasted_iota(I32, (nz * zp, xr), 1) == old) & (in_z < zr)).astype(F32).astype(BF16)
    )

    def middle(g):
        if nx > 1:
            drain(xrecv.at[pl.ds(0, (nx - 1) * xr)], x_sem.at[g])
        acc = jnp.zeros((xr, lanes_g), F32)
        for i in range(nx):
            acc = acc + xrecv[(g * nx + i) * xr : (g * nx + i + 1) * xr, :].astype(F32)
        zsend[g * nz * zp : (g + 1) * nz * zp, :] = jnp.dot(
            regroup, acc.astype(BF16), preferred_element_type=F32
        ).astype(BF16)
        mine_z = pl.ds(mo((g * nz + z) * zp, 16), zp)
        zrecv[mine_z, :] = zsend[mine_z, :]

        def pass_z(t, carry):
            hop = (t + 1) // 2
            to = lax.rem(z + nz + hop * (2 * lax.rem(t, 2) - 1), nz)
            remote(
                zsend.at[pl.ds(mo((g * nz + to) * zp, 16), zp)],
                zrecv.at[mine_z],
                z_send.at[g],
                z_sem.at[g],
                (y, to * nq + q),
            ).start()
            return carry

        lax.fori_loop(1, nz, pass_z, 0)

    def last(g):
        if nz > 1:
            drain(zrecv.at[pl.ds(0, (nz - 1) * zp)], z_sem.at[g])
        acc = jnp.zeros((zp, lanes_g), F32)
        for i in range(nz):
            acc = acc + zrecv[(g * nz + i) * zp : (g * nz + i + 1) * zp, :].astype(F32)
        for i, o in enumerate(groups(ny)[g]):
            turned = pltpu.roll(acc, lanes_g - i * half, 1) if i else acc
            slot = (sum(len(h) for h in groups(ny)[:g]) + i) * zp
            ysend[slot : slot + zp, :] = turned[:, : ysend.shape[1]].astype(BF16)
            here = yrecv.at[pl.ds(mo((y * NC + c) * zp, 16), zp)]
            mine_y = ysend.at[pl.ds(slot, zp)]
            to = shard_at(o)
            if o == 0:
                yrecv[pl.ds(mo((y * NC + c) * zp, 16), zp), :] = ysend[slot : slot + zp, :]
            else:
                remote(mine_y, here, y_sem.at[0], y_sem.at[1], (to, s)).start()
            remote(mine_y, here, y_sem.at[0], y_sem.at[1], (to, sib)).start()

    back(0)
    serve_if(4, 2)
    for g, steps in enumerate(steps_of(ny)):
        for step in steps:
            if step > 2:
                gather(step)
        if g > 0:
            back(g)
    for g in range(len(groups(ny)) - 1):
        middle(g)

    drain(ptr, pt_sem.at[1])
    drain(wf.at[pl.ds(0, (ny - 1) * half)], sib_recv)
    o0 = 1 - c

    def place_pt(yk, carry):
        pt[pl.ds(mo(yk * shard + o0 * half, 16), half), :] = ptr[pl.ds(mo(yk * half, 16), half), :]
        return carry

    lax.fori_loop(0, ny, place_pt, 0)
    pooled_rows = jnp.transpose(pt[...])
    block_w = 512 if feats % 512 == 0 else feats
    keep = used[:, 0:1] > 0.0

    def project(i, carry):
        lanes = pl.ds(mo(i * block_w, 128), block_w)
        out = jnp.dot(pooled_rows, wf[:, lanes], preferred_element_type=F32) + pbias_ref[:, lanes]
        merged_ref[:, lanes] = jnp.where(keep, out, 0.0).astype(BF16)
        return carry

    blocks = feats // block_w
    lax.fori_loop(0, blocks // 2, project, 0)

    middle(len(groups(ny)) - 1)
    for g in range(len(groups(ny)) - 1):
        last(g)
    lax.fori_loop(blocks // 2, blocks, project, 0)
    last(len(groups(ny)) - 1)
    drain(yrecv.at[pl.ds(0, (ny * NC - 1) * zp)], y_sem.at[1])
    sums = []
    for h in range(NC):
        acc = jnp.zeros((zp, yrecv.shape[1]), F32)
        for i in range(ny):
            at = (i * NC + h) * zp
            acc = acc + yrecv[at : at + zp, :].astype(F32)
        pad = jnp.zeros((zp, lanes_g - acc.shape[1]), F32)
        acc = jnp.concatenate([acc, pad], axis=1) if pad.shape[1] else acc
        lane = lax.broadcasted_iota(I32, acc.shape, 1)
        sums.append(jnp.where(lane < half, acc, 0.0))
    both = sums[0] + pltpu.roll(sums[1], half, 1)
    line = lax.broadcasted_iota(I32, both.shape, 0)
    for m in range(mper):
        for k in range(taps):
            hit = line == k * mc + c * mper + m
            one = jnp.sum(jnp.where(hit, both, 0.0), axis=0, keepdims=True)
            gw_ref[k, m : m + 1, :] = one[:, :shard]

    for way in (0, 1):
        for step in range(1, far + 1):
            for kind in (0, 1, 2):
                ring(step, way, kind).wait_send()
    drain(wf.at[pl.ds(0, (ny - 1) * half)], sib_send)
    if nx > 1:
        drain(wf.at[pl.ds(0, (ny - 1) * half), pl.ds(0, (nx - 1) * part)], share_send)
    drain(posv.at[pl.ds(0, ns - 1)], pos_sem.at[0])
    drain(arr.at[pl.ds(0, (ns - 1) * mr)], msg_sem.at[0])
    send_cot.wait_send()
    send_fr.wait_send()
    drain(pts, pt_sem.at[0])
    for g in range(len(groups(ny))):
        if nx > 1:
            drain(xrecv.at[pl.ds(0, (nx - 1) * xr)], x_send.at[g])
        if nz > 1:
            drain(zrecv.at[pl.ds(0, (nz - 1) * zp)], z_send.at[g])
    drain(yrecv.at[pl.ds(0, (ny * NC - 1) * zp)], y_sem.at[0])


def body(nx, mel_frames, positions, conv_weight, conv_bias, proj_weight, proj_bias, cotangent):
    ny, ns = lax.axis_size("dp"), lax.axis_size("seq")
    _, frames, mels = mel_frames.shape
    _, rows, feats = cotangent.shape
    taps, ch = conv_weight.shape[1:]
    tok = frames // 2
    nq = nx * NC
    nz = ns // nq
    km = taps * mels
    half = ch // ny // NC
    far = ny // 2
    n_groups = len(groups(ny))
    lanes_g = -(-max(max(len(g) for g in groups(ny)) * half, ch // ny) // 128) * 128
    lanes_y = -(-half // 128) * 128
    xr = km // nx
    zp = -(-taps * NC * (mels // ns) // 16) * 16
    cw = jnp.transpose(conv_weight, (1, 0, 2)).reshape(km, ch)
    vmem = pl.BlockSpec(memory_space=pltpu.VMEM)
    hbm = pl.BlockSpec(memory_space=pltpu.HBM)
    total = 4 * rows
    dma = pltpu.SemaphoreType.DMA
    merged, gw = pl.pallas_call(
        functools.partial(kernel, ny, ns, nx),
        out_shape=(
            jax.ShapeDtypeStruct((rows, feats), BF16),
            jax.ShapeDtypeStruct((taps, mels // ns, ch // ny), F32),
        ),
        in_specs=[hbm] * 7,
        out_specs=(vmem, vmem),
        scratch_shapes=[
            pltpu.VMEM((frames, mels), BF16),
            pltpu.VMEM((1, tok), I32),
            pltpu.VMEM((km, ch), BF16),
            pltpu.VMEM((ch,), F32),
            pltpu.VMEM((1, feats), F32),
            pltpu.VMEM((ch, feats), BF16),
            pltpu.VMEM((2 * rows, feats), BF16),
            pltpu.VMEM((ch, km), BF16),
            pltpu.VMEM((ch, 128), F32),
            pltpu.VMEM((total, mels), BF16),
            pltpu.VMEM((total, mels), BF16),
            pltpu.VMEM((ns, 1, tok), I32),
            pltpu.VMEM((4 * mels, 2 * rows), BF16),
            pltpu.VMEM((km, 4 * rows), BF16),
            pltpu.VMEM((ch, rows), BF16),
            pltpu.VMEM((ch // NC, rows), BF16),
            pltpu.VMEM((ch // NC, rows), BF16),
            pltpu.VMEM((ch // NC, 4 * rows), F32),
            pltpu.VMEM((lanes_g, 4 * rows), BF16),
            pltpu.VMEM((n_groups * km, lanes_g), BF16),
            pltpu.VMEM((n_groups * km, lanes_g), BF16),
            pltpu.VMEM((n_groups * nz * zp, lanes_g), BF16),
            pltpu.VMEM((n_groups * nz * zp, lanes_g), BF16),
            pltpu.VMEM((ny * zp, lanes_y), BF16),
            pltpu.VMEM((ny * NC * zp, lanes_y), BF16),
            dma((6 * far,)),
            dma((6 * far,)),
            dma,
            dma,
            dma,
            dma((2 * far,)),
            dma((2,)),
            dma((2,)),
            dma((2,)),
            dma((2,)),
            dma((2,)),
            dma((n_groups,)),
            dma((n_groups,)),
            dma((n_groups,)),
            dma((n_groups,)),
            dma((2,)),
            dma((7,)),
        ],
        compiler_params=pltpu.CompilerParams(
            collective_id=0, has_side_effects=True, vmem_limit_bytes=60 << 20
        ),
    )(
        mel_frames[0],
        positions,
        cw,
        conv_bias,
        proj_weight,
        proj_bias[None],
        cotangent[0],
    )
    return (merged[None], jnp.transpose(gw, (1, 0, 2)))


def solution(mesh, nx=NX):
    in_specs = (
        P("dp", "seq", None),
        P("dp", "seq"),
        P(),
        P(),
        P("dp", None),
        P(),
        P("dp", "seq", None),
    )
    out_specs = (P("dp", "seq", None), P("seq", None, "dp"))
    return jax.shard_map(
        functools.partial(body, nx), mesh=mesh, in_specs=in_specs, out_specs=out_specs, check_vma=False
    )
```

```python
import functools

import jax
import jax.numpy as jnp
from jax import lax
from jax.experimental import pallas as pl
from jax.experimental.pallas import tpu as pltpu
from jax.sharding import PartitionSpec as P

SQRT_HALF = 0.7071067811865476
INV_SQRT_TWO_PI = 0.3989422804014327
F32, BF16, I32 = jnp.float32, jnp.bfloat16, jnp.int32
MESH = pl.DeviceIdType.MESH
NT = (((1,), (1,)), ((), ()))
NX, NC = 4, 2


def mo(value, k):
    return pl.multiple_of(value, k)


def steps_of(ny):
    return {8: [[0, 1], [2], [3, 4]], 4: [[0, 1], [2]], 2: [[0], [1]]}[ny]


def groups(ny):
    far = ny // 2
    return [
        [o for t in steps for o in ([t] if t in (0, far) else [t, -t])] for steps in steps_of(ny)
    ]


def kernel(
    ny,
    ns,
    nx,
    mel_in,
    pos_in,
    cw_in,
    bias_in,
    w_ref,
    pbias_in,
    cot_ref,
    merged_ref,
    gw_ref,
    mel_ref,
    pos_ref,
    cw_ref,
    bias_ref,
    pbias_ref,
    wf,
    cot2,
    kt,
    biast,
    msgs,
    arr,
    posv,
    fr,
    xt,
    pt,
    pts,
    ptr,
    slope,
    gt,
    xsend,
    xrecv,
    zsend,
    zrecv,
    ysend,
    yrecv,
    ring_send,
    ring_recv,
    sib_send,
    sib_recv,
    share_send,
    share_recv,
    pos_sem,
    msg_sem,
    cot_sem,
    fr_sem,
    pt_sem,
    x_send,
    x_sem,
    z_send,
    z_sem,
    y_sem,
    loc_sem,
):
    nq = nx * NC
    nz = ns // nq
    frames, mels = mel_ref.shape
    tok = frames // 2
    rows = cot_ref.shape[0]
    feats = wf.shape[1]
    ch = wf.shape[0]
    shard = ch // ny
    half = shard // NC
    lanes_g = gt.shape[0]
    cap = rows // ns
    mr = 4 * cap
    km = kt.shape[1]
    taps = km // mels
    mper = mels // ns
    mc = NC * mper
    xr = km // nx
    mx = mels // nx
    zr = taps * mc
    zp = zrecv.shape[0] // (len(groups(ny)) * nz)

    y = lax.axis_index("dp")
    s = lax.axis_index("seq")
    c = lax.rem(s, NC)
    q = lax.rem(s, nq)
    z = s // nq
    x = q // NC
    sib = s + 1 - 2 * c
    up, down = lax.rem(y + 1, ny), lax.rem(y + ny - 1, ny)

    def remote(src, dst, ssem, rsem, dev):
        return pltpu.make_async_remote_copy(
            src_ref=src, dst_ref=dst, send_sem=ssem, recv_sem=rsem, device_id=dev, device_id_type=MESH
        )

    def drain(ref, sem):
        pltpu.make_async_copy(ref, ref, sem).wait()

    barrier = pltpu.get_barrier_semaphore()

    def hail_seq(i, carry):
        pl.semaphore_signal(barrier, inc=1, device_id=(y, lax.rem(s + i, ns)), device_id_type=MESH)
        return carry

    def hail_dp(i, carry):
        yt = lax.rem(y + i, ny)
        pl.semaphore_signal(barrier, inc=1, device_id=(yt, s), device_id_type=MESH)
        pl.semaphore_signal(barrier, inc=1, device_id=(yt, sib), device_id_type=MESH)
        return carry

    lax.fori_loop(1, ny, hail_dp, 0)
    lax.fori_loop(1, ns, hail_seq, 0)

    own_w = pltpu.make_async_copy(w_ref, wf.at[pl.ds(mo(y * shard, 16), shard)], loc_sem.at[0])
    own_cot = pltpu.make_async_copy(cot_ref, cot2.at[pl.ds(0, rows)], loc_sem.at[1])
    loads = [
        pltpu.make_async_copy(src, dst, loc_sem.at[2 + i])
        for i, (src, dst) in enumerate(
            [
                (pos_in, pos_ref),
                (mel_in, mel_ref),
                (cw_in, cw_ref),
                (bias_in, bias_ref),
                (pbias_in, pbias_ref),
            ]
        )
    ]
    for load in loads:
        load.start()
    own_w.start()
    own_cot.start()
    loads[0].wait()
    loads[1].wait()

    before = (
        lax.broadcasted_iota(I32, (tok, tok), 0) < lax.broadcasted_iota(I32, (tok, tok), 1)
    ).astype(BF16)
    total = ns * mr

    def spread(hit, value):
        hit_b = hit.astype(F32).astype(BF16)
        rank = jnp.dot(hit_b, before, preferred_element_type=F32)
        lane = lax.broadcasted_iota(I32, (ns, 128), 1)
        table = jnp.zeros((ns, 128), F32)
        for k in range(cap):
            entry = jnp.sum(jnp.where(hit & (rank == k), value + 1.0, 0.0), axis=1, keepdims=True)
            table = table + jnp.where(lane == k, entry, 0.0)
        group = lax.broadcasted_iota(I32, (total, ns), 0) // mr
        expand = (group == lax.broadcasted_iota(I32, (total, ns), 1)).astype(F32).astype(BF16)
        wide = jnp.dot(expand, table.astype(BF16), preferred_element_type=F32)
        n = lax.broadcasted_iota(I32, (total, 128), 0)
        chosen = lax.broadcasted_iota(I32, (total, 128), 1) == lax.rem(n // 4, cap)
        return jnp.sum(jnp.where(chosen, wide, 0.0), axis=1, keepdims=True)

    pos_row = jnp.broadcast_to(pos_ref[...], (ns, tok))
    to_dest = (pos_row // rows) == lax.broadcasted_iota(I32, (ns, tok), 0)
    token = spread(to_dest, lax.broadcasted_iota(I32, (ns, tok), 1).astype(F32))
    n_col = lax.broadcasted_iota(I32, (total, 1), 0)
    f_col = lax.rem(n_col, 4).astype(F32)
    frame = jnp.where(token > 0.0, 2.0 * (token - 1.0) - 1.0 + f_col, -100.0)
    pick = (lax.broadcasted_iota(I32, (total, frames), 1).astype(F32) == frame).astype(F32)
    p = lax.broadcasted_iota(I32, (mels, mels), 1)
    from_m = lax.rem(p // mc, nz) * (nx * mc) + (p // mx) * mc + lax.rem(p, mc)
    order = (lax.broadcasted_iota(I32, (mels, mels), 0) == from_m).astype(F32).astype(BF16)
    mel_p = jnp.dot(mel_ref[...], order, preferred_element_type=F32).astype(BF16)
    msgs[...] = jnp.dot(pick.astype(BF16), mel_p, preferred_element_type=F32).astype(BF16)
    own_slot = pl.ds(mo(s * mr, 16), mr)
    arr[own_slot, :] = msgs[own_slot, :]
    posv[s] = pos_ref[...]

    for load in loads[2:]:
        load.wait()
    for k in range(taps):
        turned = jnp.transpose(cw_ref[k * mels : (k + 1) * mels, :])
        kt[:, k * mels : (k + 1) * mels] = jnp.dot(
            turned, order, preferred_element_type=F32
        ).astype(BF16)
    for i in range(ch // 128):
        block = jnp.broadcast_to(bias_ref[128 * i : 128 * (i + 1)][None, :], (128, 128))
        biast[128 * i : 128 * (i + 1), :] = jnp.transpose(block)
    gt[...] = jnp.zeros_like(gt)

    own_w.wait()
    pl.semaphore_wait(barrier, 2 * (ny - 1) + ns - 1)

    far = ny // 2
    cut = -(-(half // 2) // 16) * 16

    shared = feats // 2
    part = shared // nx

    def wrows(owner, lo, size):
        return wf.at[pl.ds(mo(owner * shard + c * half + lo, 16), size)]

    def span(step, way):
        if step < far:
            return 0, half
        return (0, cut) if way == 0 else (cut, half - cut)

    def piece(owner, step, way, kind):
        lo, size = span(step, way)
        row = pl.ds(mo(owner * shard + c * half + lo, 16), size)
        if kind == 0:
            return wf.at[row, pl.ds(mo(shared + x * part, 128), part)]
        return wf.at[row, pl.ds((kind - 1) * (shared // 2), shared // 2)]

    def ring_sem(step, way, kind):
        return (way * far + step - 1) * 3 + kind

    def ring(step, way, kind):
        owner = lax.rem(y + ny + 1 - step if way == 0 else y + step - 1, ny)
        ref = piece(owner, step, way, kind)
        i = ring_sem(step, way, kind)
        target = (up, s) if way == 0 else (down, s)
        return remote(ref, ref, ring_send.at[i], ring_recv.at[i], target)

    def source(step, way):
        return lax.rem(y + ny - step if way == 0 else y + step, ny)

    def serve(step, kind):
        for way in (0, 1):
            ref = piece(source(step, way), step, way, kind)
            pltpu.make_async_copy(ref, ref, ring_recv.at[ring_sem(step, way, kind)]).wait()
            if step < far:
                ring(step + 1, way, kind).start()
            if kind:
                remote(ref, ref, sib_send, sib_recv, (y, sib)).start()
            else:
                for t in range(1, nx):
                    to = lax.rem(x + t, nx)
                    remote(
                        ref,
                        ref,
                        share_send,
                        share_recv.at[way * far + step - 1],
                        (y, z * nq + to * NC + c),
                    ).start()

    def gather(step):
        for way in (0, 1):
            lo, size = span(step, way)
            row = pl.ds(mo(source(step, way) * shard + c * half + lo, 16), size)
            if nx > 1:
                drain(wf.at[row, pl.ds(0, (nx - 1) * part)], share_recv.at[way * far + step - 1])
            ref = wf.at[row, pl.ds(shared, shared)]
            remote(ref, ref, sib_send, sib_recv, (y, sib)).start()

    for kind in (0, 1, 2):
        for way in (0, 1):
            ring(1, way, kind).start()

    def post(i, carry):
        hop = (i + 1) // 2
        to = lax.rem(s + ns + hop * (2 * lax.rem(i, 2) - 1), ns)
        remote(posv.at[s], posv.at[s], pos_sem.at[0], pos_sem.at[1], (y, to)).start()
        remote(
            msgs.at[pl.ds(mo(to * mr, 16), mr)],
            arr.at[pl.ds(mo(s * mr, 16), mr)],
            msg_sem.at[0],
            msg_sem.at[1],
            (y, to),
        ).start()
        return carry

    lax.fori_loop(1, ns, post, 0)
    send_cot = remote(
        cot_ref, cot2.at[pl.ds(rows, rows)], cot_sem.at[0], cot_sem.at[1], (y, sib)
    )
    send_cot.start()

    def serve_if(step, kind):
        if step <= far:
            serve(step, kind)

    serve(1, 0)
    serve(1, 1)
    serve(1, 2)
    serve_if(2, 0)
    serve_if(2, 1)
    drain(posv.at[pl.ds(0, ns - 1)], pos_sem.at[1])
    all_pos = jnp.reshape(posv[...], (ns, tok))
    mine = (all_pos // rows) == s
    slot_row = spread(mine, lax.rem(all_pos, rows).astype(F32)) - 1.0
    row_lane = lax.broadcasted_iota(I32, (total, rows), 1).astype(F32)
    at_row = row_lane == slot_row
    n_f = lax.rem(lax.broadcasted_iota(I32, (total, rows), 0), 4)
    places = [(at_row & (n_f == f)).astype(F32).astype(BF16) for f in range(4)]
    used = lax.dot_general(
        places[0], jnp.ones((total, 128), BF16), (((0,), (0,)), ((), ())), preferred_element_type=F32
    )
    drain(arr.at[pl.ds(0, (ns - 1) * mr)], msg_sem.at[1])
    arr_t = jnp.transpose(arr[...])
    for f in range(4):
        fr[f * mels : (f + 1) * mels, 0:rows] = jnp.dot(arr_t, places[f], preferred_element_type=F32).astype(BF16)
    send_fr = remote(
        fr.at[:, pl.ds(0, rows)], fr.at[:, pl.ds(rows, rows)], fr_sem.at[0], fr_sem.at[1], (y, sib)
    )
    send_fr.start()
    serve_if(2, 2)
    serve_if(3, 0)
    send_fr.wait_recv()
    wide = 2 * rows
    for j in range(2):
        for xx in range(nx):
            for k in range(taps):
                at = xx * xr + k * mx
                xt[at : at + mx, j * wide : (j + 1) * wide] = fr[
                    (j + k) * mels + xx * mx : (j + k) * mels + (xx + 1) * mx, :
                ]

    def stem(yk, carry):
        r0 = mo(yk * shard + c * half, 16)
        l0 = mo(yk * half, 16)
        weights = kt[pl.ds(r0, half), :]
        b = biast[pl.ds(r0, half), :]
        for block in range(wide // 128):
            at = block * 128
            values, slopes = [], []
            for j in range(2):
                lanes = pl.ds(j * wide + at, 128)
                window = fr[j * mels : j * mels + km, at : at + 128]
                v = jnp.dot(weights, window, preferred_element_type=F32) + b
                phi = 0.5 + 0.5 * lax.erf(v * SQRT_HALF)
                values.append(v * phi)
                slope[pl.ds(l0, half), lanes] = 0.5 * phi + v * (0.5 * INV_SQRT_TWO_PI) * jnp.exp(
                    -0.5 * v * v
                )
            pooled = (0.5 * (values[0] + values[1])).astype(BF16)
            if at < rows:
                pt[pl.ds(r0, half), at : at + 128] = pooled
            else:
                pts[pl.ds(l0, half), at - rows : at - rows + 128] = pooled
        remote(
            pts.at[pl.ds(l0, half)], ptr.at[pl.ds(l0, half)], pt_sem.at[0], pt_sem.at[1], (y, sib)
        ).start()
        return carry

    serve_if(3, 1)
    gather(1)
    serve_if(4, 0)
    lax.fori_loop(0, ny // 4, stem, 0)
    serve_if(3, 2)
    if far > 1:
        gather(2)
    lax.fori_loop(ny // 4, ny - ny // 4, stem, 0)
    serve_if(4, 1)
    lax.fori_loop(ny - ny // 4, ny, stem, 0)
    own_cot.wait()
    send_cot.wait_recv()

    def shard_at(offset):
        return lax.rem(y + ny + offset, ny)

    def back(g):
        offsets = groups(ny)[g]
        w = jnp.concatenate([wrows(shard_at(o), 0, half)[...] for o in offsets], axis=0)
        gp = lax.dot_general(w, cot2[...], NT, preferred_element_type=F32).astype(BF16).astype(F32)
        for i, o in enumerate(offsets):
            l0 = mo(shard_at(o) * half, 16)
            for j in range(2):
                lanes = slice(j * wide, (j + 1) * wide)
                grad = gp[i * half : (i + 1) * half] * slope[pl.ds(l0, half), lanes]
                gt[i * half : (i + 1) * half, lanes] = grad.astype(BF16)
        product = lax.dot_general(xt[...], gt[...], NT, preferred_element_type=F32)
        xsend[g * km : (g + 1) * km, :] = product.astype(BF16)
        mine_x = pl.ds(mo((g * nx + x) * xr, 16), xr)
        xrecv[mine_x, :] = xsend[pl.ds(mo(g * km + x * xr, 16), xr), :]

        def pass_x(t, carry):
            back_t = nx - t
            hop = (back_t + 1) // 2
            to = lax.rem(x + nx + hop * (2 * lax.rem(back_t, 2) - 1), nx)
            remote(
                xsend.at[pl.ds(mo(g * km + to * xr, 16), xr)],
                xrecv.at[mine_x],
                x_send.at[g],
                x_sem.at[g],
                (y, z * nq + to * NC + c),
            ).start()
            return carry

        lax.fori_loop(1, nx, pass_x, 0)

    n_new = lax.broadcasted_iota(I32, (nz * zp, xr), 0)
    in_z = lax.rem(n_new, zp)
    old = (in_z // mc) * mx + (n_new // zp) * mc + lax.rem(in_z, mc)
    regroup = (
        ((lax.broadcasted_iota(I32, (nz * zp, xr), 1) == old) & (in_z < zr)).astype(F32).astype(BF16)
    )

    def middle(g):
        if nx > 1:
            drain(xrecv.at[pl.ds(0, (nx - 1) * xr)], x_sem.at[g])
        acc = jnp.zeros((xr, lanes_g), F32)
        for i in range(nx):
            acc = acc + xrecv[(g * nx + i) * xr : (g * nx + i + 1) * xr, :].astype(F32)
        zsend[g * nz * zp : (g + 1) * nz * zp, :] = jnp.dot(
            regroup, acc.astype(BF16), preferred_element_type=F32
        ).astype(BF16)
        mine_z = pl.ds(mo((g * nz + z) * zp, 16), zp)
        zrecv[mine_z, :] = zsend[mine_z, :]

        def pass_z(t, carry):
            back_t = nz - t
            hop = (back_t + 1) // 2
            to = lax.rem(z + nz + hop * (2 * lax.rem(back_t, 2) - 1), nz)
            remote(
                zsend.at[pl.ds(mo((g * nz + to) * zp, 16), zp)],
                zrecv.at[mine_z],
                z_send.at[g],
                z_sem.at[g],
                (y, to * nq + q),
            ).start()
            return carry

        lax.fori_loop(1, nz, pass_z, 0)

    def last(g):
        if nz > 1:
            drain(zrecv.at[pl.ds(0, (nz - 1) * zp)], z_sem.at[g])
        acc = jnp.zeros((zp, lanes_g), F32)
        for i in range(nz):
            acc = acc + zrecv[(g * nz + i) * zp : (g * nz + i + 1) * zp, :].astype(F32)
        for i, o in enumerate(groups(ny)[g]):
            turned = pltpu.roll(acc, lanes_g - i * half, 1) if i else acc
            slot = (sum(len(h) for h in groups(ny)[:g]) + i) * zp
            ysend[slot : slot + zp, :] = turned[:, : ysend.shape[1]].astype(BF16)
            here = yrecv.at[pl.ds(mo((y * NC + c) * zp, 16), zp)]
            mine_y = ysend.at[pl.ds(slot, zp)]
            to = shard_at(o)
            if o == 0:
                yrecv[pl.ds(mo((y * NC + c) * zp, 16), zp), :] = ysend[slot : slot + zp, :]
            else:
                remote(mine_y, here, y_sem.at[0], y_sem.at[1], (to, s)).start()
            remote(mine_y, here, y_sem.at[0], y_sem.at[1], (to, sib)).start()

    back(0)
    serve_if(4, 2)
    for g, steps in enumerate(steps_of(ny)):
        for step in steps:
            if step > 2:
                gather(step)
        if g > 0:
            back(g)
    for g in range(len(groups(ny)) - 1):
        middle(g)

    drain(ptr, pt_sem.at[1])
    drain(wf.at[pl.ds(0, (ny - 1) * half)], sib_recv)
    o0 = 1 - c

    def place_pt(yk, carry):
        pt[pl.ds(mo(yk * shard + o0 * half, 16), half), :] = ptr[pl.ds(mo(yk * half, 16), half), :]
        return carry

    lax.fori_loop(0, ny, place_pt, 0)
    pooled_rows = jnp.transpose(pt[...])
    block_w = 512 if feats % 512 == 0 else feats
    keep = used[:, 0:1] > 0.0

    def project(i, carry):
        lanes = pl.ds(mo(i * block_w, 128), block_w)
        out = jnp.dot(pooled_rows, wf[:, lanes], preferred_element_type=F32) + pbias_ref[:, lanes]
        merged_ref[:, lanes] = jnp.where(keep, out, 0.0).astype(BF16)
        return carry

    blocks = feats // block_w
    lax.fori_loop(0, blocks // 2, project, 0)

    middle(len(groups(ny)) - 1)
    for g in range(len(groups(ny)) - 1):
        last(g)
    lax.fori_loop(blocks // 2, blocks, project, 0)
    last(len(groups(ny)) - 1)
    drain(yrecv.at[pl.ds(0, (ny * NC - 1) * zp)], y_sem.at[1])
    sums = []
    for h in range(NC):
        acc = jnp.zeros((zp, yrecv.shape[1]), F32)
        for i in range(ny):
            at = (i * NC + h) * zp
            acc = acc + yrecv[at : at + zp, :].astype(F32)
        pad = jnp.zeros((zp, lanes_g - acc.shape[1]), F32)
        acc = jnp.concatenate([acc, pad], axis=1) if pad.shape[1] else acc
        lane = lax.broadcasted_iota(I32, acc.shape, 1)
        sums.append(jnp.where(lane < half, acc, 0.0))
    both = sums[0] + pltpu.roll(sums[1], half, 1)
    line = lax.broadcasted_iota(I32, both.shape, 0)
    for m in range(mper):
        for k in range(taps):
            hit = line == k * mc + c * mper + m
            one = jnp.sum(jnp.where(hit, both, 0.0), axis=0, keepdims=True)
            gw_ref[k, m : m + 1, :] = one[:, :shard]

    for way in (0, 1):
        for step in range(1, far + 1):
            for kind in (0, 1, 2):
                ring(step, way, kind).wait_send()
    drain(wf.at[pl.ds(0, (ny - 1) * half)], sib_send)
    if nx > 1:
        drain(wf.at[pl.ds(0, (ny - 1) * half), pl.ds(0, (nx - 1) * part)], share_send)
    drain(posv.at[pl.ds(0, ns - 1)], pos_sem.at[0])
    drain(arr.at[pl.ds(0, (ns - 1) * mr)], msg_sem.at[0])
    send_cot.wait_send()
    send_fr.wait_send()
    drain(pts, pt_sem.at[0])
    for g in range(len(groups(ny))):
        if nx > 1:
            drain(xrecv.at[pl.ds(0, (nx - 1) * xr)], x_send.at[g])
        if nz > 1:
            drain(zrecv.at[pl.ds(0, (nz - 1) * zp)], z_send.at[g])
    drain(yrecv.at[pl.ds(0, (ny * NC - 1) * zp)], y_sem.at[0])


def body(nx, mel_frames, positions, conv_weight, conv_bias, proj_weight, proj_bias, cotangent):
    ny, ns = lax.axis_size("dp"), lax.axis_size("seq")
    _, frames, mels = mel_frames.shape
    _, rows, feats = cotangent.shape
    taps, ch = conv_weight.shape[1:]
    tok = frames // 2
    nq = nx * NC
    nz = ns // nq
    km = taps * mels
    half = ch // ny // NC
    far = ny // 2
    n_groups = len(groups(ny))
    lanes_g = -(-max(max(len(g) for g in groups(ny)) * half, ch // ny) // 128) * 128
    lanes_y = -(-half // 128) * 128
    xr = km // nx
    zp = -(-taps * NC * (mels // ns) // 16) * 16
    cw = jnp.transpose(conv_weight, (1, 0, 2)).reshape(km, ch)
    vmem = pl.BlockSpec(memory_space=pltpu.VMEM)
    hbm = pl.BlockSpec(memory_space=pltpu.HBM)
    total = 4 * rows
    dma = pltpu.SemaphoreType.DMA
    merged, gw = pl.pallas_call(
        functools.partial(kernel, ny, ns, nx),
        out_shape=(
            jax.ShapeDtypeStruct((rows, feats), BF16),
            jax.ShapeDtypeStruct((taps, mels // ns, ch // ny), F32),
        ),
        in_specs=[hbm] * 7,
        out_specs=(vmem, vmem),
        scratch_shapes=[
            pltpu.VMEM((frames, mels), BF16),
            pltpu.VMEM((1, tok), I32),
            pltpu.VMEM((km, ch), BF16),
            pltpu.VMEM((ch,), F32),
            pltpu.VMEM((1, feats), F32),
            pltpu.VMEM((ch, feats), BF16),
            pltpu.VMEM((2 * rows, feats), BF16),
            pltpu.VMEM((ch, km), BF16),
            pltpu.VMEM((ch, 128), F32),
            pltpu.VMEM((total, mels), BF16),
            pltpu.VMEM((total, mels), BF16),
            pltpu.VMEM((ns, 1, tok), I32),
            pltpu.VMEM((4 * mels, 2 * rows), BF16),
            pltpu.VMEM((km, 4 * rows), BF16),
            pltpu.VMEM((ch, rows), BF16),
            pltpu.VMEM((ch // NC, rows), BF16),
            pltpu.VMEM((ch // NC, rows), BF16),
            pltpu.VMEM((ch // NC, 4 * rows), F32),
            pltpu.VMEM((lanes_g, 4 * rows), BF16),
            pltpu.VMEM((n_groups * km, lanes_g), BF16),
            pltpu.VMEM((n_groups * km, lanes_g), BF16),
            pltpu.VMEM((n_groups * nz * zp, lanes_g), BF16),
            pltpu.VMEM((n_groups * nz * zp, lanes_g), BF16),
            pltpu.VMEM((ny * zp, lanes_y), BF16),
            pltpu.VMEM((ny * NC * zp, lanes_y), BF16),
            dma((6 * far,)),
            dma((6 * far,)),
            dma,
            dma,
            dma,
            dma((2 * far,)),
            dma((2,)),
            dma((2,)),
            dma((2,)),
            dma((2,)),
            dma((2,)),
            dma((n_groups,)),
            dma((n_groups,)),
            dma((n_groups,)),
            dma((n_groups,)),
            dma((2,)),
            dma((7,)),
        ],
        compiler_params=pltpu.CompilerParams(
            collective_id=0, has_side_effects=True, vmem_limit_bytes=60 << 20
        ),
    )(
        mel_frames[0],
        positions,
        cw,
        conv_bias,
        proj_weight,
        proj_bias[None],
        cotangent[0],
    )
    return (merged[None], jnp.transpose(gw, (1, 0, 2)))


def solution(mesh, nx=NX):
    in_specs = (
        P("dp", "seq", None),
        P("dp", "seq"),
        P(),
        P(),
        P("dp", None),
        P(),
        P("dp", "seq", None),
    )
    out_specs = (P("dp", "seq", None), P("seq", None, "dp"))
    return jax.shard_map(
        functools.partial(body, nx), mesh=mesh, in_specs=in_specs, out_specs=out_specs, check_vma=False
    )
```
